32 devices in a mesh: wide: 8 (over z, x), bulk: 4 (over y, core).
Axes of the slice: x: 2, y: 2, z: 4, core: 2. Of those that a mesh axis runs over, the one named last changes fastest.
Arguments:
- fields: float32 [1024, 6, 512], P(('wide', 'bulk')), may hold values from -6 to 6
- scales: float32 [1024, 3], P(('wide', 'bulk')), may hold values from 1 to 3
- class_table: float32 [8, 2], replicated, may hold values from 1 to 4
- material: int32 [1024], P(('wide', 'bulk')), may hold values from 0 to 7, as said below
- neighbour_class: int32 [1024, 6], P(('wide', 'bulk')), may hold values from 0 to 7, as said below
- orientation: int32 [1024, 6], P(('wide', 'bulk')), may hold values from 0 to 7
- face_source: int32 [1024, 6], P(('wide', 'bulk')), may hold values from -1 to 287, as said below
- wide_send: int32 [8, 4, 4, 16], P('wide', 'bulk'), may hold values from -1 to 191, as said below
- bulk_send: int32 [8, 4, 2, 16], P('wide', 'bulk'), may hold values from -1 to 191, as said below
Outputs:
- new_fields: float32 [1024, 6, 512], P(('wide', 'bulk'))
The draws below stay inside these ranges and needn't reach their ends.
Inputs may be any that keep to these rules, and one draw needn't show every extreme that they name: `material`: classes of elements; class 0 and class 7 occur in every draw. `neighbour_class`: for a face whose source is an own face or a received trace row, the material class of the element that trace belongs to; for a boundary face, the element's own class. `face_source`: rows 0 .. 191 are the device's own faces, the next 64 rows what arrived over wide (16 for each offset -2, -1, +1, +2 in order), then 16 rows from the previous and 16 from the next index of bulk. Every received row that carries a trace is named by exactly one face of the receiving device, rows from -1 entries by none; no face names itself; some faces are boundary faces. `wide_send`: Element-face numbers of the sending device; a device shares faces over wide only with the indices at offsets -2, -1, +1 and +2 (cyclic); in each block of 16 entries the used entries come first and -1 fills the rest; every block holds at least one entry, and every device fills all 16 entries for offset +1. `bulk_send`: Element-face numbers of the sending device; used entries first, then -1; every row holds at least one entry and some rows of every draw are full.
All inputs are finite; a program needn't handle non-finite values.
Results may differ from the reference program's by a relative error of at most 0.00005.
Values sent between devices are 32-bit elements; how exact they have to be, the bound alone decides.
A program may use at most 64 MiB of HBM per device.

```python
import math
import jax
import jax.numpy as jnp
import numpy as np
from jax import lax

E_DEV = 32
NODES = 512
FIELDS = 6
CLASSES = 8
SLOT = 16
BSLOT = 16
ELEMS = 1024
N_WIDE = 8
N_BULK = 4


WIDE_OFFSETS = (-2, -1, 1, 2)


def draw_layout(key):
    faces = 6 * E_DEV
    recv_rows = 4 * SLOT + 2 * BSLOT
    keys = jax.random.split(jax.random.fold_in(key, 4242), 8)
    material = jax.random.randint(keys[0], (N_WIDE, N_BULK, E_DEV), 0, CLASSES)
    material = material.at[0, 0, 0].set(CLASSES - 1).at[0, 0, 1].set(0)
    wide_count = jax.random.randint(keys[1], (N_WIDE, N_BULK, 4), 1, SLOT + 1)
    wide_count = wide_count.at[:, :, 2].set(SLOT)
    wide_face = jax.random.randint(keys[2], (N_WIDE, N_BULK, 4, SLOT), 0, faces)
    wide_face = wide_face.at[0, 0, 2, 0].set(faces - 1)
    slot_pos = jnp.arange(SLOT, dtype=jnp.int32)
    wide_used = slot_pos < wide_count[..., None]
    wide_send = jnp.where(wide_used, wide_face, -1)
    bulk_count = jax.random.randint(keys[3], (N_WIDE, N_BULK, 2), 1, BSLOT + 1)
    position_sum = jnp.arange(N_WIDE, dtype=jnp.int32)[:, None, None] + jnp.arange(N_BULK, dtype=jnp.int32)[None, :, None] + jnp.arange(2, dtype=jnp.int32)[None, None, :]
    bulk_count = jnp.where(position_sum % 3 == 0, BSLOT, bulk_count)
    bulk_face = jax.random.randint(keys[4], (N_WIDE, N_BULK, 2, BSLOT), 0, faces)
    bulk_face = bulk_face.at[0, 0, 0, 0].set(faces - 1)
    bulk_pos = jnp.arange(BSLOT, dtype=jnp.int32)
    bulk_send = jnp.where(bulk_pos < bulk_count[..., None], bulk_face, -1)
    wide_valid = jnp.concatenate([jnp.roll(wide_used[:, :, place], offset, axis=0) for place, offset in enumerate(WIDE_OFFSETS)], axis=2)
    below_valid = jnp.roll(bulk_pos < bulk_count[:, :, 1, None], 1, axis=1)
    above_valid = jnp.roll(bulk_pos < bulk_count[:, :, 0, None], -1, axis=1)
    incoming_valid = jnp.concatenate([wide_valid, below_valid, above_valid], axis=2)
    incoming_code = faces + jnp.broadcast_to(jnp.arange(recv_rows, dtype=jnp.int32), (N_WIDE, N_BULK, recv_rows))
    filler = jnp.where(jax.random.randint(keys[5], (N_WIDE, N_BULK, faces), 0, 4) == 0, -1, -3)
    filler = filler.at[:, :, 0].set(-1).at[:, :, 1].set(-3)
    codes = jnp.concatenate([jnp.where(incoming_valid, incoming_code, -2), filler], axis=2)
    ranks = jnp.concatenate([jnp.where(incoming_valid, 0, 2), jnp.ones((N_WIDE, N_BULK, faces), jnp.int32)], axis=2)
    order = jnp.argsort(ranks, axis=2, stable=True)[:, :, :faces]
    chosen = jnp.take_along_axis(codes, order, axis=2)
    shuffled = jax.random.permutation(keys[6], chosen, axis=2, independent=True)
    face_id = jnp.arange(faces, dtype=jnp.int32)
    offsets = jax.random.randint(keys[7], (N_WIDE, N_BULK, faces), 1, faces)
    face_source = jnp.where(shuffled == -3, (face_id + offsets) % faces, shuffled)
    face_class = jnp.repeat(material, 6, axis=2)
    wide_class = jnp.take_along_axis(face_class, jnp.maximum(wide_send, 0).reshape(N_WIDE, N_BULK, 4 * SLOT), axis=2)
    wide_class = wide_class.reshape(N_WIDE, N_BULK, 4, SLOT)
    wide_class = jnp.concatenate([jnp.roll(wide_class[:, :, place], offset, axis=0) for place, offset in enumerate(WIDE_OFFSETS)], axis=2)
    bulk_class = jnp.take_along_axis(face_class, jnp.maximum(bulk_send, 0).reshape(N_WIDE, N_BULK, 2 * BSLOT), axis=2)
    bulk_class = bulk_class.reshape(N_WIDE, N_BULK, 2, BSLOT)
    below_class = jnp.roll(bulk_class[:, :, 1], 1, axis=1)
    above_class = jnp.roll(bulk_class[:, :, 0], -1, axis=1)
    table_class = jnp.concatenate([face_class, wide_class, below_class, above_class], axis=2)
    neighbour = jnp.take_along_axis(table_class, jnp.maximum(face_source, 0), axis=2)
    neighbour = jnp.where(face_source < 0, face_class, neighbour)
    return (material, neighbour, face_source, wide_send, bulk_send)


def draw_material(key, part):
    return draw_layout(key)[0].reshape(ELEMS).astype(jnp.int32)


def draw_neighbour_class(key, part):
    return draw_layout(key)[1].reshape(ELEMS, 6).astype(jnp.int32)


def draw_face_source(key, part):
    return draw_layout(key)[2].reshape(ELEMS, 6).astype(jnp.int32)


def draw_wide_send(key, part):
    return draw_layout(key)[3].astype(jnp.int32)


def draw_bulk_send(key, part):
    return draw_layout(key)[4].astype(jnp.int32)


def with_ends(result, stream_key, least, largest):
    spot = [jax.random.randint(jax.random.fold_in(stream_key, axis), (), 0, length) for axis, length in enumerate(result.shape)]
    widest = result.shape.index(max(result.shape))
    beside = spot[:widest] + [(spot[widest] + 1) % result.shape[widest]] + spot[widest + 1:]
    return result.at[tuple(spot)].set(least).at[tuple(beside)].set(largest)


def levels(rng, dims, cuts, low, high):
    loudness = 1.0
    for dim, blocks in cuts:
        steps = jax.random.uniform(jax.random.fold_in(jax.random.fold_in(rng, 6), dim), (blocks,), jnp.float32, low / len(cuts), high / len(cuts))
        loudness = loudness * jnp.repeat(jnp.exp(steps), dims[dim] // blocks).reshape((-1,) + (1,) * (len(dims) - 1 - dim))
    return loudness


def normal_values(key, shape, width, most, cuts=(), kind=jnp.bfloat16):
    gain = levels(key, shape, cuts, -0.22, 0.18) if cuts else 1.0
    entries = jax.random.normal(key, shape, jnp.float32) * width * gain
    return jnp.minimum(jnp.maximum(entries, -most), most).astype(kind)


def setup_inputs(seed: int = 0) -> dict:
    seeds = jax.random.split(jax.random.key(seed), 10)
    return {
        "fields": normal_values(seeds[0], (ELEMS, FIELDS, NODES), 1.0, 6.0, ((0, 32),), jnp.float32),
        "scales": jnp.clip(jnp.exp(math.log(3.0) - 1.0986123 * jax.random.uniform(seeds[1], (ELEMS, 3), jnp.float32) ** levels(seeds[1], (ELEMS, 3), ((0, 32),), -0.2, 0.2)), 1.0, 3.0),
        "class_table": jnp.clip(jnp.exp(jax.random.uniform(seeds[2], (CLASSES, 2), jnp.float32, math.log(1.0), math.log(4.0))), 1.0, 4.0),
        "material": draw_material(jax.random.fold_in(seeds[9], 71), 0),
        "neighbour_class": draw_neighbour_class(jax.random.fold_in(seeds[9], 71), 0),
        "orientation": with_ends(jax.random.randint(seeds[5], (ELEMS, 6), 0, 8), jax.random.fold_in(seeds[5], 1), 0, 7).astype(jnp.int32),
        "face_source": draw_face_source(jax.random.fold_in(seeds[9], 71), 0),
        "wide_send": draw_wide_send(jax.random.fold_in(seeds[9], 71), 0),
        "bulk_send": draw_bulk_send(jax.random.fold_in(seeds[9], 71), 0),
    }


TIME_STEP = 0.005
LIFT_WEIGHT = 28.0
WIDE_OFFSETS = (-2, -1, 1, 2)

def legendre_value(degree, point):
    previous = 1.0
    current = point
    for order in range(1, degree):
        following = ((2 * order + 1) * point * current - order * previous) / (order + 1)
        previous = current
        current = following
    return current

def gll_matrix():
    degree = 7
    points = [-1.0, -0.8717401485096066, -0.5917001814331423, -0.2092992179024789, 0.2092992179024789, 0.5917001814331423, 0.8717401485096066, 1.0]
    values = [legendre_value(degree, point) for point in points]
    matrix = np.zeros((degree + 1, degree + 1))
    for row_index in range(degree + 1):
        for col_index in range(degree + 1):
            if row_index != col_index:
                matrix[row_index, col_index] = values[row_index] / (values[col_index] * (points[row_index] - points[col_index]))
    matrix[0, 0] = -degree * (degree + 1) / 4.0
    matrix[degree, degree] = degree * (degree + 1) / 4.0
    return jnp.asarray(matrix, dtype=jnp.float32)

def lookup(indices, values):
    onehot = indices[..., None] == jnp.arange(values.shape[0], dtype=jnp.int32)
    return lax.optimization_barrier(jnp.sum(jnp.where(onehot, values, 0.0), axis=-1))

def face_place(face):
    axis_id = face // 2
    return (slice(None), slice(None)) + (slice(None),) * axis_id + (7 * (face % 2),)

def face_tiles(cube):
    return jnp.stack([cube[face_place(face)] for face in range(6)], axis=1)

def exterior(tiles, rows, face_source, orientation):
    flags = orientation[:, :, None, None, None]
    turned = jnp.where(flags & 4 > 0, jnp.swapaxes(rows, -1, -2), rows)
    turned = jnp.where(flags & 1 > 0, jnp.flip(turned, -2), turned)
    turned = jnp.where(flags & 2 > 0, jnp.flip(turned, -1), turned)
    signs = jnp.array([-1.0, -1.0, -1.0, 1.0, 1.0, 1.0], dtype=jnp.float32)
    mirror = tiles * signs[:, None, None]
    return jnp.where(face_source[:, :, None, None, None] < 0, mirror, turned)

def cross_normal(axis_id, sign, first, second, third):
    blank = jnp.zeros_like(first)
    if axis_id == 0:
        return (blank, -sign * third, sign * second)
    if axis_id == 1:
        return (sign * third, blank, -sign * first)
    return (-sign * second, sign * first, blank)

def derive(values, matrix, axis_id):
    forms = ('ij,ejyz->eiyz', 'ij,exjz->exiz', 'ij,exyj->exyi')
    return jnp.einsum(forms[axis_id], matrix, values, precision=lax.Precision.HIGHEST)

def field_rate(cube, tiles, scales, permit, permea, own_imp, outside, outside_imp):
    matrix = gll_matrix()

    def slope(component, axis_id):
        return derive(cube[:, component], matrix, axis_id) * scales[:, axis_id][:, None, None, None]
    curl_h = (slope(5, 1) - slope(4, 2), slope(3, 2) - slope(5, 0), slope(4, 0) - slope(3, 1))
    curl_e = (slope(2, 1) - slope(1, 2), slope(0, 2) - slope(2, 0), slope(1, 0) - slope(0, 1))
    inv_eps = (1.0 / permit)[:, None, None, None]
    inv_mu = (1.0 / permea)[:, None, None, None]
    rate = jnp.stack([entry * inv_eps for entry in curl_h] + [-entry * inv_mu for entry in curl_e], axis=1)
    for face in range(6):
        axis_id = face // 2
        sign = 2.0 * (face % 2) - 1.0
        jump = tiles[:, face] - outside[:, face]
        z_in = own_imp[:, None, None]
        z_out = outside_imp[:, face][:, None, None]
        cross_e = cross_normal(axis_id, sign, jump[:, 0], jump[:, 1], jump[:, 2])
        cross_h = cross_normal(axis_id, sign, jump[:, 3], jump[:, 4], jump[:, 5])
        e_inner = [z_out * jump[:, 3 + component] - cross_e[component] for component in range(3)]
        h_inner = [jump[:, component] / z_out + cross_h[component] for component in range(3)]
        flux_e = cross_normal(axis_id, sign, e_inner[0], e_inner[1], e_inner[2])
        flux_h = cross_normal(axis_id, sign, h_inner[0], h_inner[1], h_inner[2])
        lift = LIFT_WEIGHT * scales[:, axis_id][:, None, None]
        e_factor = -lift / (permit[:, None, None] * (z_in + z_out))
        h_factor = lift / (permea[:, None, None] * (1.0 / z_in + 1.0 / z_out))
        face_rate = jnp.stack([e_factor * entry for entry in flux_e] + [h_factor * entry for entry in flux_h], axis=1)
        rate = rate.at[face_place(face)].add(face_rate)
    return rate

def pick_batched(traces, index):
    got = jnp.take_along_axis(traces, jnp.maximum(index, 0)[..., None], axis=2)
    return jnp.where((index >= 0)[..., None], got, 0.0)

def by_wide(array):
    return array.reshape((N_WIDE, -1) + array.shape[1:])

def reference(fields, scales, class_table, material, neighbour_class, orientation, face_source, wide_send, bulk_send):
    faces = 6 * E_DEV
    imped_table = jnp.sqrt(class_table[:, 1] / class_table[:, 0])
    permit = lookup(material, class_table[:, 0])
    permea = lookup(material, class_table[:, 1])
    own_imp = lookup(material, imped_table)
    outside_imp = lookup(neighbour_class, imped_table)

    def block_rate(pieces):
        return field_rate(*pieces)

    def rate_of(state):
        cube = state.reshape(ELEMS, 6, 8, 8, 8)
        tiles = face_tiles(cube)
        traces = tiles.reshape(N_WIDE, N_BULK, faces, 384)
        sent = pick_batched(traces, wide_send.reshape(N_WIDE, N_BULK, 4 * SLOT))
        sent = sent.reshape(N_WIDE, N_BULK, 4, SLOT, 384)
        received = jnp.concatenate([jnp.roll(sent[:, :, place], offset, axis=0) for place, offset in enumerate(WIDE_OFFSETS)], axis=2)
        bulk_rows = pick_batched(traces, bulk_send.reshape(N_WIDE, N_BULK, 2 * BSLOT))
        bulk_rows = bulk_rows.reshape(N_WIDE, N_BULK, 2, BSLOT, 384)
        below = jnp.roll(bulk_rows[:, :, 1], 1, axis=1)
        above = jnp.roll(bulk_rows[:, :, 0], -1, axis=1)
        table = jnp.concatenate([traces, received, below, above], axis=2)
        index = jnp.maximum(face_source, 0).reshape(N_WIDE, N_BULK, faces, 1)
        rows = jnp.take_along_axis(table, index, axis=2).reshape(ELEMS, 6, 6, 8, 8)
        outside = exterior(tiles, rows, face_source, orientation)
        pieces = tuple((by_wide(array) for array in (cube, tiles, scales, permit, permea, own_imp, outside, outside_imp)))
        return lax.map(block_rate, pieces).reshape(ELEMS, 6, 512)
    first = rate_of(fields)
    second = rate_of(fields + TIME_STEP * first)
    return fields + 0.5 * TIME_STEP * (first + second)
```

```python
import functools

import jax
import jax.numpy as jnp
import numpy as np
from jax import lax
from jax.experimental import pallas as pl
from jax.experimental.pallas import tpu as pltpu
from jax.sharding import PartitionSpec as P

TIME_STEP = 0.005
LIFT_WEIGHT = 28.0
WIDE_OFFSETS = (-2, -1, 1, 2)
MESH = pl.DeviceIdType.MESH
F32 = jnp.float32
BF16 = jnp.bfloat16


def legendre_value(degree, point):
    previous = 1.0
    current = point
    for order in range(1, degree):
        following = ((2 * order + 1) * point * current - order * previous) / (order + 1)
        previous = current
        current = following
    return current


def gll_numpy():
    degree = 7
    points = [
        -1.0,
        -0.8717401485096066,
        -0.5917001814331423,
        -0.2092992179024789,
        0.2092992179024789,
        0.5917001814331423,
        0.8717401485096066,
        1.0,
    ]
    values = [legendre_value(degree, point) for point in points]
    matrix = np.zeros((degree + 1, degree + 1))
    for row_index in range(degree + 1):
        for col_index in range(degree + 1):
            if row_index != col_index:
                matrix[row_index, col_index] = values[row_index] / (
                    values[col_index] * (points[row_index] - points[col_index])
                )
    matrix[0, 0] = -degree * (degree + 1) / 4.0
    matrix[degree, degree] = degree * (degree + 1) / 4.0
    return matrix


def face_nodes():
    nodes = np.zeros((6, 64), dtype=np.int64)
    for face in range(6):
        axis_id = face // 2
        level = 7 * (face % 2)
        for place in range(64):
            outer = place // 8
            inner = place % 8
            if axis_id == 0:
                coords = (level, outer, inner)
            elif axis_id == 1:
                coords = (outer, level, inner)
            else:
                coords = (outer, inner, level)
            nodes[face, place] = 64 * coords[0] + 8 * coords[1] + coords[2]
    return nodes


def halves(matrix):
    high = np.asarray(matrix, dtype=np.float32).astype(jnp.bfloat16)
    low = (matrix - high.astype(np.float64)).astype(np.float32).astype(jnp.bfloat16)
    return high, low


def constants(elems):
    pick = np.zeros((512, 384), dtype=np.float32)
    pick[face_nodes().reshape(-1), np.arange(384)] = 1.0
    turned = gll_numpy().T
    eye = np.eye(8)
    first = np.kron(turned, np.eye(64))
    second = np.kron(np.eye(2), np.kron(turned, eye))
    third = np.kron(np.eye(16), turned)
    d0 = np.stack(halves(first))
    d12 = np.concatenate([second, third], axis=1)
    high, low = halves(d12)
    d12 = np.concatenate([high, high, low], axis=0)
    turn = np.zeros((128, 8, 128), dtype=np.float32)
    for flag in range(8):
        for place in range(64):
            outer, inner = place // 8, place % 8
            outer = 7 - outer if flag & 1 else outer
            inner = 7 - inner if flag & 2 else inner
            source = inner * 8 + outer if flag & 4 else outer * 8 + inner
            for half in range(2):
                turn[half * 64 + source, flag, half * 64 + place] = 1.0
    turn = turn.reshape(128, 1024)
    turn = np.concatenate([turn, turn], axis=0)
    code = np.zeros((1, 6 * elems), dtype=np.float32)
    for face in range(6):
        code[0, face * elems : (face + 1) * elems] = 6 * np.arange(elems) + face
    return (
        jnp.asarray(pick, dtype=BF16),
        jnp.asarray(pick.T, dtype=BF16),
        jnp.asarray(d0),
        jnp.asarray(d12),
        jnp.asarray(turn, dtype=BF16),
        jnp.asarray(code),
    )


def split(value):
    high = value.astype(BF16)
    low = (value - high.astype(F32)).astype(BF16)
    return high, low


def mul(left, right):
    return jnp.dot(left, right, preferred_element_type=F32)


def column(row):
    size = row.shape[1]
    shape = (size, size)
    same = lax.broadcasted_iota(jnp.int32, shape, 0) == lax.broadcasted_iota(jnp.int32, shape, 1)
    return jnp.sum(jnp.where(same, jnp.broadcast_to(row, shape), 0.0), axis=1, keepdims=True)


def swap(value):
    return pltpu.roll(value, 64, 1)


def kernel(
    fields_ref,
    scales_ref,
    class_ref,
    material_ref,
    neighbour_ref,
    orient_ref,
    source_ref,
    wide_ref,
    bulk_ref,
    pick_ref,
    lift_ref,
    d0_ref,
    d12_ref,
    turn_ref,
    code_ref,
    out_ref,
    state_ref,
    rate_ref,
    table_ref,
    own_ref,
    far_ref,
    choose_ref,
    coef_ref,
    send_ref,
    recv_ref,
    send_sem,
    recv_sem,
):
    elems = fields_ref.shape[0]
    faces = 6 * elems
    slot = wide_ref.shape[3]
    wide_id, bulk_id = lax.axis_index("wide"), lax.axis_index("bulk")
    n_wide, n_bulk = lax.axis_size("wide"), lax.axis_size("bulk")
    targets = [(lax.rem(wide_id + offset + n_wide, n_wide), bulk_id) for offset in WIDE_OFFSETS]
    targets.append((wide_id, lax.rem(bulk_id + 1, n_bulk)))
    targets.append((wide_id, lax.rem(bulk_id + n_bulk - 1, n_bulk)))

    barrier = pltpu.get_barrier_semaphore()
    for target in targets:
        pl.semaphore_signal(barrier, inc=1, device_id=target, device_id_type=MESH)

    for comp in range(6):
        state_ref[comp * elems : (comp + 1) * elems, :] = fields_ref[:, comp, :]

    code = code_ref[...]
    wide_rows = wide_ref[0, 0].astype(F32)
    bulk_rows = bulk_ref[0, 0].astype(F32)
    order = [wide_rows[q : q + 1] for q in range(4)] + [bulk_rows[1:2], bulk_rows[0:1]]
    for q, row in enumerate(order):
        choose_ref[q * slot : (q + 1) * slot, :] = jnp.where(column(row) == code, 1.0, 0.0).astype(BF16)

    low_half = lax.broadcasted_iota(jnp.int32, (elems, 128), 1) < 64
    source = source_ref[...].astype(F32)
    far_code = (lax.broadcasted_iota(jnp.int32, (elems, 6 * slot), 1) + faces).astype(F32)
    material = column(material_ref[...].astype(F32))
    neighbour = neighbour_ref[...]
    table = class_ref[...]
    imped = jnp.sqrt(table[:, 1:2] / table[:, 0:1])
    permit = jnp.zeros((elems, 1), F32)
    permea = jnp.zeros((elems, 1), F32)
    own_imp = jnp.zeros((elems, 1), F32)
    z_all = jnp.zeros((elems, 6), F32)
    for entry in range(class_ref.shape[0]):
        hit = material == float(entry)
        permit = permit + jnp.where(hit, table[entry : entry + 1, 0:1], 0.0)
        permea = permea + jnp.where(hit, table[entry : entry + 1, 1:2], 0.0)
        own_imp = own_imp + jnp.where(hit, imped[entry : entry + 1, :], 0.0)
        z_all = z_all + jnp.where(neighbour == entry, imped[entry : entry + 1, :], 0.0)
    inv_eps = 1.0 / permit
    inv_mu = 1.0 / permea
    scale = [scales_ref[:, axis : axis + 1] for axis in range(3)]
    for face in range(6):
        rows = slice(face * elems, (face + 1) * elems)
        sign = 2.0 * (face % 2) - 1.0
        origin = source[:, face : face + 1]
        own_ref[rows, :] = jnp.where(origin == code, 1.0, 0.0).astype(BF16)
        far_ref[rows, :] = jnp.where(origin == far_code, 1.0, 0.0).astype(BF16)
        z_out = z_all[:, face : face + 1]
        lift = LIFT_WEIGHT * scale[face // 2]
        e_factor = -lift / (permit * (own_imp + z_out))
        h_factor = lift / (permea * (1.0 / own_imp + 1.0 / z_out))
        coef_ref[0, rows, :] = jnp.where(low_half, e_factor, -h_factor)
        coef_ref[1, rows, :] = jnp.where(low_half, -sign * z_out * e_factor, -sign * h_factor / z_out)
        coef_ref[2, rows, :] = jnp.where(origin < 0.0, jnp.where(low_half, 2.0, 0.0), 1.0)
    orient = orient_ref[...]

    pl.semaphore_wait(barrier, len(targets))

    def stage(number):
        state = state_ref[...]
        high, low = split(state)
        pick = pick_ref[...]
        traces = mul(high, pick) + mul(low, pick)
        half = lax.broadcasted_iota(jnp.int32, (3 * elems, 128), 1) < 64
        for axis in range(3):
            e_part = traces[0 : 3 * elems, axis * 128 : (axis + 1) * 128]
            h_part = traces[3 * elems :, axis * 128 : (axis + 1) * 128]
            near = jnp.where(half, e_part, swap(h_part))
            away = jnp.where(half, swap(e_part), h_part)
            for side, part in enumerate((near, away)):
                first = (2 * axis + side) * elems
                for dim in range(3):
                    table_ref[first : first + elems, dim * 128 : (dim + 1) * 128] = part[
                        dim * elems : (dim + 1) * elems
                    ]
        tab_high, tab_low = split(table_ref[...])
        choose = choose_ref[...]
        sent = mul(choose, tab_high) + mul(choose, tab_low)
        copies = []
        for q, target in enumerate(targets):
            send_ref[number, q] = sent[q * slot : (q + 1) * slot]
        for q, target in enumerate(targets):
            copy = pltpu.make_async_remote_copy(
                src_ref=send_ref.at[number, q],
                dst_ref=recv_ref.at[number, q],
                send_sem=send_sem.at[number, q],
                recv_sem=recv_sem.at[number, q],
                device_id=target,
                device_id_type=MESH,
            )
            copy.start()
            copies.append(copy)

        slope0 = mul(high, d0_ref[0]) + mul(low, d0_ref[0]) + mul(high, d0_ref[1])
        wide_in = jnp.concatenate(
            [
                jnp.concatenate([part[:, block * 128 : (block + 1) * 128] for block in range(4)], axis=0)
                for part in (high, low, high)
            ],
            axis=1,
        )
        slope12 = mul(wide_in, d12_ref[...])

        def slope(comp, axis):
            if axis == 0:
                return slope0[comp * elems : (comp + 1) * elems]
            lanes = slice((axis - 1) * 128, axis * 128)
            return jnp.concatenate(
                [
                    slope12[(block * 6 + comp) * elems : (block * 6 + comp + 1) * elems, lanes]
                    for block in range(4)
                ],
                axis=1,
            )

        volume = []
        for field in range(2):
            other = 3 * (1 - field)
            factor = inv_eps if field == 0 else -inv_mu
            for dim in range(3):
                one, two = (dim + 1) % 3, (dim + 2) % 3
                volume.append(
                    (factor * scale[one]) * slope(other + two, one)
                    - (factor * scale[two]) * slope(other + one, two)
                )
        volume = jnp.concatenate(volume, axis=0)

        own = own_ref[...]
        got_high = mul(own, tab_high)
        got_low = mul(own, tab_low)
        for copy in copies:
            copy.wait()
        far_high, far_low = split(recv_ref[number].reshape(6 * slot, 384))
        far = far_ref[...]
        got_high = (got_high + mul(far, far_high)).astype(BF16)
        got_low = (got_low + mul(far, far_low)).astype(BF16)

        pieces = []
        for face in range(6):
            rows = slice(face * elems, (face + 1) * elems)
            for step in (1, 2):
                dim = (face // 2 + step) % 3
                lanes = slice(dim * 128, (dim + 1) * 128)
                pieces.append(jnp.concatenate([got_high[rows, lanes], got_low[rows, lanes]], axis=1))
        turned = mul(jnp.concatenate(pieces, axis=0), turn_ref[...])

        faces_out = {}
        for face in range(6):
            axis = face // 2
            rows = slice(face * elems, (face + 1) * elems)
            flag = jnp.broadcast_to(orient[:, face : face + 1], (elems, 128))
            jumps = []
            for step in (1, 2):
                dim = (axis + step) % 3
                first = (2 * face + step - 1) * elems
                forms = [turned[first : first + elems, o * 128 : (o + 1) * 128] for o in range(8)]
                for bit in (1, 2, 4):
                    chosen = (flag & bit) > 0
                    forms = [
                        jnp.where(chosen, forms[2 * o + 1], forms[2 * o]) for o in range(len(forms) // 2)
                    ]
                own_trace = table_ref[rows, dim * 128 : (dim + 1) * 128]
                jumps.append(own_trace * coef_ref[2, rows, :] - forms[0])
            straight = coef_ref[0, rows, :]
            crossed = coef_ref[1, rows, :]
            faces_out[face, (axis + 1) % 3] = straight * jumps[0] + crossed * swap(jumps[1])
            faces_out[face, (axis + 2) % 3] = straight * jumps[1] - crossed * swap(jumps[0])

        blank = jnp.zeros((elems, 128), F32)
        lines = []
        for field in range(2):
            for dim in range(3):
                line = []
                for axis in range(3):
                    if axis == dim:
                        line.append(blank)
                        continue
                    near, away = faces_out[2 * axis, dim], faces_out[2 * axis + 1, dim]
                    if field == 0:
                        line.append(jnp.where(low_half, near, swap(away)))
                    else:
                        line.append(jnp.where(low_half, swap(near), away))
                lines.append(jnp.concatenate(line, axis=1))
        lift_high, lift_low = split(jnp.concatenate(lines, axis=0))
        lift = lift_ref[...]
        return volume + mul(lift_high, lift) + mul(lift_low, lift)

    first = stage(0)
    rate_ref[...] = first
    state_ref[...] = state_ref[...] + TIME_STEP * first
    second = stage(1)
    total = rate_ref[...] + second
    for comp in range(6):
        rows = slice(comp * elems, (comp + 1) * elems)
        out_ref[:, comp, :] = fields_ref[:, comp, :] + 0.5 * TIME_STEP * total[rows]


def local(
    fields,
    scales,
    class_table,
    material,
    neighbour_class,
    orientation,
    face_source,
    wide_send,
    bulk_send,
):
    elems = fields.shape[0]
    slot = wide_send.shape[3]
    faces = 6 * elems
    vmem = pl.BlockSpec(memory_space=pltpu.VMEM)
    return pl.pallas_call(
        kernel,
        out_shape=jax.ShapeDtypeStruct(fields.shape, fields.dtype),
        in_specs=[vmem] * 15,
        out_specs=vmem,
        scratch_shapes=[
            pltpu.VMEM((faces, 512), F32),
            pltpu.VMEM((faces, 512), F32),
            pltpu.VMEM((faces, 384), F32),
            pltpu.VMEM((faces, faces), BF16),
            pltpu.VMEM((faces, 6 * slot), BF16),
            pltpu.VMEM((6 * slot, faces), BF16),
            pltpu.VMEM((3, faces, 128), F32),
            pltpu.VMEM((2, 6, slot, 384), F32),
            pltpu.VMEM((2, 6, slot, 384), F32),
            pltpu.SemaphoreType.DMA((2, 6)),
            pltpu.SemaphoreType.DMA((2, 6)),
        ],
        compiler_params=pltpu.CompilerParams(
            collective_id=0, has_side_effects=True, vmem_limit_bytes=48 * 1024 * 1024
        ),
    )(
        fields,
        scales,
        class_table,
        material.reshape(1, elems),
        neighbour_class,
        orientation,
        face_source,
        wide_send,
        bulk_send,
        *constants(elems),
    )


def solution(mesh):
    in_specs = (
        P(("wide", "bulk"), None, None),
        P(("wide", "bulk"), None),
        P(),
        P(("wide", "bulk")),
        P(("wide", "bulk"), None),
        P(("wide", "bulk"), None),
        P(("wide", "bulk"), None),
        P("wide", "bulk", None, None),
        P("wide", "bulk", None, None),
    )
    out_specs = P(("wide", "bulk"), None, None)
    return jax.shard_map(local, mesh=mesh, in_specs=in_specs, out_specs=out_specs, check_vma=False)
```

```python
import functools

import jax
import jax.numpy as jnp
import numpy as np
from jax import lax
from jax.experimental import pallas as pl
from jax.experimental.pallas import tpu as pltpu
from jax.sharding import PartitionSpec as P

TIME_STEP = 0.005
LIFT_WEIGHT = 28.0
WIDE_OFFSETS = (-2, -1, 1, 2)
MESH = pl.DeviceIdType.MESH
F32 = jnp.float32
BF16 = jnp.bfloat16


def legendre_value(degree, point):
    previous = 1.0
    current = point
    for order in range(1, degree):
        following = ((2 * order + 1) * point * current - order * previous) / (order + 1)
        previous = current
        current = following
    return current


def gll_numpy():
    degree = 7
    points = [
        -1.0,
        -0.8717401485096066,
        -0.5917001814331423,
        -0.2092992179024789,
        0.2092992179024789,
        0.5917001814331423,
        0.8717401485096066,
        1.0,
    ]
    values = [legendre_value(degree, point) for point in points]
    matrix = np.zeros((degree + 1, degree + 1))
    for row_index in range(degree + 1):
        for col_index in range(degree + 1):
            if row_index != col_index:
                matrix[row_index, col_index] = values[row_index] / (
                    values[col_index] * (points[row_index] - points[col_index])
                )
    matrix[0, 0] = -degree * (degree + 1) / 4.0
    matrix[degree, degree] = degree * (degree + 1) / 4.0
    return matrix


def face_nodes():
    nodes = np.zeros((6, 64), dtype=np.int64)
    for face in range(6):
        axis_id = face // 2
        level = 7 * (face % 2)
        for place in range(64):
            outer = place // 8
            inner = place % 8
            if axis_id == 0:
                coords = (level, outer, inner)
            elif axis_id == 1:
                coords = (outer, level, inner)
            else:
                coords = (outer, inner, level)
            nodes[face, place] = 64 * coords[0] + 8 * coords[1] + coords[2]
    return nodes


def halves(matrix):
    high = np.asarray(matrix, dtype=np.float32).astype(jnp.bfloat16)
    low = (matrix - high.astype(np.float64)).astype(np.float32).astype(jnp.bfloat16)
    return high, low


def constants(elems):
    pick = np.zeros((512, 384), dtype=np.float32)
    pick[face_nodes().reshape(-1), np.arange(384)] = 1.0
    turned = gll_numpy().T
    eye = np.eye(8)
    first = np.kron(turned, np.eye(64))
    second = np.kron(np.eye(2), np.kron(turned, eye))
    third = np.kron(np.eye(16), turned)
    d0 = np.stack(halves(first))
    d12 = np.concatenate([second, third], axis=1)
    high, low = halves(d12)
    d12 = np.concatenate([high, high, low], axis=0)
    turn = np.zeros((128, 8, 128), dtype=np.float32)
    for flag in range(8):
        for place in range(64):
            outer, inner = place // 8, place % 8
            outer = 7 - outer if flag & 1 else outer
            inner = 7 - inner if flag & 2 else inner
            source = inner * 8 + outer if flag & 4 else outer * 8 + inner
            for half in range(2):
                turn[half * 64 + source, flag, half * 64 + place] = 1.0
    turn = turn.reshape(128, 1024)
    turn = np.concatenate([turn, turn], axis=0)
    code = np.zeros((1, 6 * elems), dtype=np.float32)
    for face in range(6):
        code[0, face * elems : (face + 1) * elems] = 6 * np.arange(elems) + face
    return (
        jnp.asarray(pick, dtype=BF16),
        jnp.asarray(pick.T, dtype=BF16),
        jnp.asarray(d0),
        jnp.asarray(d12),
        jnp.asarray(turn, dtype=BF16),
        jnp.asarray(code),
    )


def split(value):
    high = value.astype(BF16)
    low = (value - high.astype(F32)).astype(BF16)
    return high, low


def mul(left, right):
    return jnp.dot(left, right, preferred_element_type=F32)


def column(row):
    size = row.shape[1]
    shape = (size, size)
    same = lax.broadcasted_iota(jnp.int32, shape, 0) == lax.broadcasted_iota(jnp.int32, shape, 1)
    return jnp.sum(jnp.where(same, jnp.broadcast_to(row, shape), 0.0), axis=1, keepdims=True)


def swap(value):
    return pltpu.roll(value, 64, 1)


def kernel(
    fields_hbm,
    scales_ref,
    class_ref,
    material_ref,
    neighbour_ref,
    orient_ref,
    source_ref,
    wide_ref,
    bulk_ref,
    pick_hbm,
    lift_hbm,
    d0_hbm,
    d12_hbm,
    turn_hbm,
    code_ref,
    out_ref,
    state_ref,
    base_ref,
    pick_ref,
    lift_ref,
    d0_ref,
    d12_ref,
    turn_ref,
    small_ref,
    table_ref,
    own_ref,
    far_ref,
    choose_ref,
    coef_ref,
    send_ref,
    recv_ref,
    load_sem,
    send_sem,
    recv_sem,
):
    elems = material_ref.shape[1]
    faces = 6 * elems
    slot = wide_ref.shape[3]
    wide_id, bulk_id = lax.axis_index("wide"), lax.axis_index("bulk")
    n_wide, n_bulk = lax.axis_size("wide"), lax.axis_size("bulk")
    targets = [(lax.rem(wide_id + offset + n_wide, n_wide), bulk_id) for offset in WIDE_OFFSETS]
    targets.append((wide_id, lax.rem(bulk_id + 1, n_bulk)))
    targets.append((wide_id, lax.rem(bulk_id + n_bulk - 1, n_bulk)))

    barrier = pltpu.get_barrier_semaphore()
    for target in targets:
        pl.semaphore_signal(barrier, inc=1, device_id=target, device_id_type=MESH)

    loads = []
    for place, (source, target) in enumerate(
        (
            (fields_hbm, state_ref),
            (pick_hbm, pick_ref),
            (d0_hbm, d0_ref),
            (d12_hbm, d12_ref),
            (turn_hbm, turn_ref),
            (lift_hbm, lift_ref),
        )
    ):
        load = pltpu.make_async_copy(source, target, load_sem.at[place])
        load.start()
        loads.append(load)

    code = code_ref[...]
    wide_rows = wide_ref[0, 0].astype(F32)
    bulk_rows = bulk_ref[0, 0].astype(F32)
    order = [wide_rows[q : q + 1] for q in range(4)] + [bulk_rows[1:2], bulk_rows[0:1]]
    for q, row in enumerate(order):
        choose_ref[q * slot : (q + 1) * slot, :] = jnp.where(column(row) == code, 1.0, 0.0).astype(BF16)

    low_half = lax.broadcasted_iota(jnp.int32, (elems, 128), 1) < 64
    far_code = (lax.broadcasted_iota(jnp.int32, (elems, 6 * slot), 1) + faces).astype(F32)
    material = material_ref[...]
    neighbour = neighbour_ref[...]
    table = class_ref[...]
    imped = jnp.sqrt(table[1:2, :] / table[0:1, :])
    permit = jnp.zeros((1, elems), F32)
    permea = jnp.zeros((1, elems), F32)
    own_imp = jnp.zeros((1, elems), F32)
    z_out = jnp.zeros((6, elems), F32)
    for entry in range(class_ref.shape[1]):
        hit = material == entry
        permit = permit + jnp.where(hit, table[0:1, entry : entry + 1], 0.0)
        permea = permea + jnp.where(hit, table[1:2, entry : entry + 1], 0.0)
        own_imp = own_imp + jnp.where(hit, imped[:, entry : entry + 1], 0.0)
        z_out = z_out + jnp.where(neighbour == entry, imped[:, entry : entry + 1], 0.0)
    side = lax.broadcasted_iota(jnp.int32, (6, elems), 0)
    sign = jnp.where((side & 1) > 0, 1.0, -1.0)
    scales = scales_ref[...]
    lift = LIFT_WEIGHT * jnp.where(side < 2, scales[0:1], jnp.where(side < 4, scales[1:2], scales[2:3]))
    e_factor = -lift / (permit * (own_imp + z_out))
    h_factor = lift / (permea * (1.0 / own_imp + 1.0 / z_out))
    small_ref[...] = jnp.zeros_like(small_ref)
    small_ref[0:6, 0:elems] = source_ref[...].astype(F32)
    small_ref[8:14, 0:elems] = orient_ref[...].astype(F32)
    small_ref[16:22, 0:elems] = e_factor
    small_ref[24:30, 0:elems] = -h_factor
    small_ref[32:38, 0:elems] = -sign * z_out * e_factor
    small_ref[40:46, 0:elems] = -sign * h_factor / z_out
    small_ref[48:51, 0:elems] = scales / permit
    small_ref[56:59, 0:elems] = -scales / permea
    columns = jnp.transpose(small_ref[...])[0:elems]

    def col(group, index):
        return columns[:, 8 * group + index : 8 * group + index + 1]

    flags = []
    for face in range(6):
        rows = slice(face * elems, (face + 1) * elems)
        origin = col(0, face)
        own_ref[rows, :] = jnp.where(origin == code, 1.0, 0.0).astype(BF16)
        far_ref[rows, :] = jnp.where(origin == far_code, 1.0, 0.0).astype(BF16)
        coef_ref[0, rows, :] = jnp.where(low_half, col(2, face), col(3, face))
        coef_ref[1, rows, :] = jnp.where(low_half, col(4, face), col(5, face))
        coef_ref[2, rows, :] = jnp.where(origin < 0.0, jnp.where(low_half, 2.0, 0.0), 1.0)
        coef_ref[3, rows, :] = jnp.broadcast_to(col(1, face), (elems, 128))

    pl.semaphore_wait(barrier, len(targets))

    def stage(number):
        if number == 0:
            loads[0].wait()
            loads[1].wait()
        high, low = split(state_ref[...])
        both = mul(jnp.concatenate([high, low], axis=0), pick_ref[...])
        traces = both[0:faces] + both[faces:]
        half = lax.broadcasted_iota(jnp.int32, (3 * elems, 128), 1) < 64
        for axis in range(3):
            e_part = traces[0 : 3 * elems, axis * 128 : (axis + 1) * 128]
            h_part = traces[3 * elems :, axis * 128 : (axis + 1) * 128]
            near = jnp.where(half, e_part, swap(h_part))
            away = jnp.where(half, swap(e_part), h_part)
            for side, part in enumerate((near, away)):
                first = (2 * axis + side) * elems
                for dim in range(3):
                    table_ref[first : first + elems, dim * 128 : (dim + 1) * 128] = part[
                        dim * elems : (dim + 1) * elems
                    ]
        tab = jnp.concatenate(split(table_ref[...]), axis=1)
        sent = mul(choose_ref[...], tab)
        sent = sent[:, 0:384] + sent[:, 384:]
        copies = []
        for q, target in enumerate(targets):
            send_ref[number, q] = sent[q * slot : (q + 1) * slot]
        for q, target in enumerate(targets):
            copy = pltpu.make_async_remote_copy(
                src_ref=send_ref.at[number, q],
                dst_ref=recv_ref.at[number, q],
                send_sem=send_sem.at[number, q],
                recv_sem=recv_sem.at[number, q],
                device_id=target,
                device_id_type=MESH,
            )
            copy.start()
            copies.append(copy)

        if number == 0:
            loads[2].wait()
            loads[3].wait()
        active = jnp.concatenate([high[elems : 3 * elems], high[4 * elems :]], axis=0)
        active_low = jnp.concatenate([low[elems : 3 * elems], low[4 * elems :]], axis=0)
        slope0 = mul(jnp.concatenate([active, active_low], axis=0), d0_ref[0])
        slope0 = slope0[0 : 4 * elems] + slope0[4 * elems :] + mul(active, d0_ref[1])
        wide_in = jnp.concatenate(
            [
                jnp.concatenate([part[:, block * 128 : (block + 1) * 128] for block in range(4)], axis=0)
                for part in (high, low, high)
            ],
            axis=1,
        )
        slope12 = mul(wide_in, d12_ref[...])

        def slope(comp, axis):
            if axis == 0:
                place = 2 * (comp // 3) + comp % 3 - 1
                return slope0[place * elems : (place + 1) * elems]
            lanes = slice((axis - 1) * 128, axis * 128)
            return jnp.concatenate(
                [
                    slope12[(block * 6 + comp) * elems : (block * 6 + comp + 1) * elems, lanes]
                    for block in range(4)
                ],
                axis=1,
            )

        volume = []
        for field in range(2):
            other = 3 * (1 - field)
            for dim in range(3):
                one, two = (dim + 1) % 3, (dim + 2) % 3
                volume.append(
                    col(6 + field, one) * slope(other + two, one)
                    - col(6 + field, two) * slope(other + one, two)
                )
        volume = jnp.concatenate(volume, axis=0)

        got = mul(own_ref[...], tab)
        if number == 0:
            loads[4].wait()
            loads[5].wait()
        for copy in copies:
            copy.wait()
        beyond = jnp.concatenate(split(recv_ref[number].reshape(6 * slot, 384)), axis=1)
        got = (got + mul(far_ref[...], beyond)).astype(BF16)

        pieces = []
        for face in range(6):
            rows = slice(face * elems, (face + 1) * elems)
            for step in (1, 2):
                dim = (face // 2 + step) % 3
                pieces.append(
                    jnp.concatenate(
                        [
                            got[rows, dim * 128 : (dim + 1) * 128],
                            got[rows, 384 + dim * 128 : 384 + (dim + 1) * 128],
                        ],
                        axis=1,
                    )
                )
        turned = mul(jnp.concatenate(pieces, axis=0), turn_ref[...])

        faces_out = {}
        for face in range(6):
            axis = face // 2
            rows = slice(face * elems, (face + 1) * elems)
            flag = coef_ref[3, rows, :].astype(jnp.int32)
            jumps = []
            for step in (1, 2):
                dim = (axis + step) % 3
                first = (2 * face + step - 1) * elems
                forms = [turned[first : first + elems, o * 128 : (o + 1) * 128] for o in range(8)]
                for bit in (1, 2, 4):
                    chosen = (flag & bit) > 0
                    forms = [
                        jnp.where(chosen, forms[2 * o + 1], forms[2 * o]) for o in range(len(forms) // 2)
                    ]
                own_trace = table_ref[rows, dim * 128 : (dim + 1) * 128]
                jumps.append(own_trace * coef_ref[2, rows, :] - forms[0])
            straight = coef_ref[0, rows, :]
            crossed = coef_ref[1, rows, :]
            faces_out[face, (axis + 1) % 3] = straight * jumps[0] + crossed * swap(jumps[1])
            faces_out[face, (axis + 2) % 3] = straight * jumps[1] - crossed * swap(jumps[0])

        blank = jnp.zeros((elems, 128), F32)
        lines = []
        for field in range(2):
            for dim in range(3):
                line = []
                for axis in range(3):
                    if axis == dim:
                        line.append(blank)
                        continue
                    near, away = faces_out[2 * axis, dim], faces_out[2 * axis + 1, dim]
                    if field == 0:
                        line.append(jnp.where(low_half, near, swap(away)))
                    else:
                        line.append(jnp.where(low_half, swap(near), away))
                lines.append(jnp.concatenate(line, axis=1))
        lifted = mul(jnp.concatenate(split(jnp.concatenate(lines, axis=0)), axis=0), lift_ref[...])
        return volume + (lifted[0:faces] + lifted[faces:])

    first = stage(0)
    state = state_ref[...]
    base_ref[...] = state + (0.5 * TIME_STEP) * first
    state_ref[...] = state + TIME_STEP * first
    second = stage(1)
    out_ref[...] = base_ref[...] + (0.5 * TIME_STEP) * second


def local(
    fields,
    scales,
    class_table,
    material,
    neighbour_class,
    orientation,
    face_source,
    wide_send,
    bulk_send,
):
    elems = fields.shape[0]
    slot = wide_send.shape[3]
    faces = 6 * elems
    vmem = pl.BlockSpec(memory_space=pltpu.VMEM)
    hbm = pl.BlockSpec(memory_space=pltpu.HBM)
    matrices = constants(elems)
    result = pl.pallas_call(
        kernel,
        out_shape=jax.ShapeDtypeStruct((faces, 512), F32),
        in_specs=[hbm] + [vmem] * 8 + [hbm] * 5 + [vmem],
        out_specs=vmem,
        scratch_shapes=[
            pltpu.VMEM((faces, 512), F32),
            pltpu.VMEM((faces, 512), F32),
            *[pltpu.VMEM(matrix.shape, BF16) for matrix in matrices[:5]],
            pltpu.VMEM((128, 128), F32),
            pltpu.VMEM((faces, 384), F32),
            pltpu.VMEM((faces, faces), BF16),
            pltpu.VMEM((faces, 6 * slot), BF16),
            pltpu.VMEM((6 * slot, faces), BF16),
            pltpu.VMEM((4, faces, 128), F32),
            pltpu.VMEM((2, 6, slot, 384), F32),
            pltpu.VMEM((2, 6, slot, 384), F32),
            pltpu.SemaphoreType.DMA((6,)),
            pltpu.SemaphoreType.DMA((2, 6)),
            pltpu.SemaphoreType.DMA((2, 6)),
        ],
        compiler_params=pltpu.CompilerParams(
            collective_id=0, has_side_effects=True, vmem_limit_bytes=67043328
        ),
    )(
        fields.transpose(1, 0, 2).reshape(faces, 512),
        scales.T,
        class_table.T,
        material.reshape(1, elems),
        neighbour_class.T,
        orientation.T,
        face_source.T,
        wide_send,
        bulk_send,
        *matrices,
    )
    return result.reshape(6, elems, 512).transpose(1, 0, 2)


def solution(mesh):
    in_specs = (
        P(("wide", "bulk"), None, None),
        P(("wide", "bulk"), None),
        P(),
        P(("wide", "bulk")),
        P(("wide", "bulk"), None),
        P(("wide", "bulk"), None),
        P(("wide", "bulk"), None),
        P("wide", "bulk", None, None),
        P("wide", "bulk", None, None),
    )
    out_specs = P(("wide", "bulk"), None, None)
    return jax.shard_map(local, mesh=mesh, in_specs=in_specs, out_specs=out_specs, check_vma=False)
```

```python
import functools

import jax
import jax.numpy as jnp
import numpy as np
from jax import lax
from jax.experimental import pallas as pl
from jax.experimental.pallas import tpu as pltpu
from jax.sharding import PartitionSpec as P

TIME_STEP = 0.005
LIFT_WEIGHT = 28.0
WIDE_OFFSETS = (-2, -1, 1, 2)
MESH = pl.DeviceIdType.MESH
F32 = jnp.float32
BF16 = jnp.bfloat16


def legendre_value(degree, point):
    previous = 1.0
    current = point
    for order in range(1, degree):
        following = ((2 * order + 1) * point * current - order * previous) / (order + 1)
        previous = current
        current = following
    return current


def gll_numpy():
    degree = 7
    points = [
        -1.0,
        -0.8717401485096066,
        -0.5917001814331423,
        -0.2092992179024789,
        0.2092992179024789,
        0.5917001814331423,
        0.8717401485096066,
        1.0,
    ]
    values = [legendre_value(degree, point) for point in points]
    matrix = np.zeros((degree + 1, degree + 1))
    for row_index in range(degree + 1):
        for col_index in range(degree + 1):
            if row_index != col_index:
                matrix[row_index, col_index] = values[row_index] / (
                    values[col_index] * (points[row_index] - points[col_index])
                )
    matrix[0, 0] = -degree * (degree + 1) / 4.0
    matrix[degree, degree] = degree * (degree + 1) / 4.0
    return matrix


def face_nodes():
    nodes = np.zeros((6, 64), dtype=np.int64)
    for face in range(6):
        axis_id = face // 2
        level = 7 * (face % 2)
        for place in range(64):
            outer = place // 8
            inner = place % 8
            if axis_id == 0:
                coords = (level, outer, inner)
            elif axis_id == 1:
                coords = (outer, level, inner)
            else:
                coords = (outer, inner, level)
            nodes[face, place] = 64 * coords[0] + 8 * coords[1] + coords[2]
    return nodes


def halves(matrix):
    high = np.asarray(matrix, dtype=np.float32).astype(jnp.bfloat16)
    low = (matrix - high.astype(np.float64)).astype(np.float32).astype(jnp.bfloat16)
    return high, low


def constants():
    pick = np.zeros((512, 384), dtype=np.float32)
    pick[face_nodes().reshape(-1), np.arange(384)] = 1.0
    turned = gll_numpy().T
    eye = np.eye(8)
    first = np.kron(turned, np.eye(64))
    second = np.kron(np.eye(2), np.kron(turned, eye))
    third = np.kron(np.eye(16), turned)
    d0 = np.stack(halves(first))
    d12 = np.concatenate([second, third], axis=1)
    high, low = halves(d12)
    d12 = np.concatenate([high, high, low], axis=0)
    turn = np.zeros((128, 8, 128), dtype=np.float32)
    for flag in range(8):
        for place in range(64):
            outer, inner = place // 8, place % 8
            outer = 7 - outer if flag & 1 else outer
            inner = 7 - inner if flag & 2 else inner
            source = inner * 8 + outer if flag & 4 else outer * 8 + inner
            for half in range(2):
                turn[half * 64 + source, flag, half * 64 + place] = 1.0
    turn = turn.reshape(128, 1024)
    turn = np.concatenate([turn, turn], axis=0)
    return (
        jnp.asarray(pick, dtype=BF16),
        jnp.asarray(pick.T, dtype=BF16),
        jnp.asarray(d0),
        jnp.asarray(d12),
        jnp.asarray(turn, dtype=BF16),
    )


def split(value):
    high = value.astype(BF16)
    low = (value - high.astype(F32)).astype(BF16)
    return high, low


def mul(left, right):
    return jnp.dot(left, right, preferred_element_type=F32)


def column(row):
    size = row.shape[1]
    shape = (size, size)
    same = lax.broadcasted_iota(jnp.int32, shape, 0) == lax.broadcasted_iota(jnp.int32, shape, 1)
    return jnp.sum(jnp.where(same, jnp.broadcast_to(row, shape), 0.0), axis=1, keepdims=True)


def swap(value):
    return pltpu.roll(value, 64, 1)


def kernel(
    fields_hbm,
    scales_hbm,
    class_hbm,
    material_hbm,
    neighbour_hbm,
    orient_hbm,
    source_hbm,
    wide_hbm,
    bulk_hbm,
    pick_hbm,
    lift_hbm,
    d0_hbm,
    d12_hbm,
    turn_hbm,
    out_ref,
    state_ref,
    base_ref,
    pick_ref,
    lift_ref,
    d0_ref,
    d12_ref,
    turn_ref,
    scales_ref,
    class_ref,
    material_ref,
    neighbour_ref,
    orient_ref,
    source_ref,
    wide_ref,
    bulk_ref,
    small_ref,
    table_ref,
    own_ref,
    far_ref,
    choose_ref,
    coef_ref,
    curl_ref,
    send_ref,
    recv_ref,
    load_sem,
    send_sem,
    recv_sem,
):
    elems = material_hbm.shape[1]
    faces = 6 * elems
    slot = wide_hbm.shape[3]
    wide_id, bulk_id = lax.axis_index("wide"), lax.axis_index("bulk")
    n_wide, n_bulk = lax.axis_size("wide"), lax.axis_size("bulk")
    targets = [(lax.rem(wide_id + offset + n_wide, n_wide), bulk_id) for offset in WIDE_OFFSETS]
    targets.append((wide_id, lax.rem(bulk_id + 1, n_bulk)))
    targets.append((wide_id, lax.rem(bulk_id + n_bulk - 1, n_bulk)))

    barrier = pltpu.get_barrier_semaphore()
    for target in targets:
        pl.semaphore_signal(barrier, inc=1, device_id=target, device_id_type=MESH)

    loads = {}
    for place, (name, source, target) in enumerate(
        (
            ("wide", wide_hbm, wide_ref),
            ("bulk", bulk_hbm, bulk_ref),
            ("fields", fields_hbm, state_ref),
            ("pick", pick_hbm, pick_ref),
            ("scales", scales_hbm, scales_ref),
            ("class", class_hbm, class_ref),
            ("material", material_hbm, material_ref),
            ("neighbour", neighbour_hbm, neighbour_ref),
            ("orient", orient_hbm, orient_ref),
            ("source", source_hbm, source_ref),
            ("d0", d0_hbm, d0_ref),
            ("d12", d12_hbm, d12_ref),
            ("turn", turn_hbm, turn_ref),
            ("lift", lift_hbm, lift_ref),
        )
    ):
        loads[name] = pltpu.make_async_copy(source, target, load_sem.at[place])
        loads[name].start()

    spot = lax.broadcasted_iota(jnp.int32, (1, faces), 1)
    part = jnp.zeros((1, faces), jnp.int32)
    for face in range(1, 6):
        part = part + jnp.where(spot >= face * elems, 1, 0)
    code = (6 * (spot - elems * part) + part).astype(F32)
    loads["wide"].wait()
    loads["bulk"].wait()
    wide_rows = wide_ref[0, 0].astype(F32)
    bulk_rows = bulk_ref[0, 0].astype(F32)
    order = [wide_rows[q : q + 1] for q in range(4)] + [bulk_rows[1:2], bulk_rows[0:1]]
    for q, row in enumerate(order):
        choose_ref[q * slot : (q + 1) * slot, :] = jnp.where(column(row) == code, 1.0, 0.0).astype(BF16)

    low_half = lax.broadcasted_iota(jnp.int32, (elems, 128), 1) < 64

    def prepare():
        for name in ("scales", "class", "material", "neighbour", "orient", "source"):
            loads[name].wait()
        far_code = (lax.broadcasted_iota(jnp.int32, (elems, 6 * slot), 1) + faces).astype(F32)
        material = material_ref[...]
        neighbour = neighbour_ref[...]
        table = class_ref[...]
        imped = jnp.sqrt(table[1:2, :] / table[0:1, :])
        permit = jnp.zeros((1, elems), F32)
        permea = jnp.zeros((1, elems), F32)
        own_imp = jnp.zeros((1, elems), F32)
        z_out = jnp.zeros((6, elems), F32)
        for entry in range(class_ref.shape[1]):
            hit = material == entry
            permit = permit + jnp.where(hit, table[0:1, entry : entry + 1], 0.0)
            permea = permea + jnp.where(hit, table[1:2, entry : entry + 1], 0.0)
            own_imp = own_imp + jnp.where(hit, imped[:, entry : entry + 1], 0.0)
            z_out = z_out + jnp.where(neighbour == entry, imped[:, entry : entry + 1], 0.0)
        side = lax.broadcasted_iota(jnp.int32, (6, elems), 0)
        sign = jnp.where((side & 1) > 0, 1.0, -1.0)
        scales = scales_ref[...]
        lift = LIFT_WEIGHT * jnp.where(side < 2, scales[0:1], jnp.where(side < 4, scales[1:2], scales[2:3]))
        e_factor = -lift / (permit * (own_imp + z_out))
        h_factor = lift / (permea * (1.0 / own_imp + 1.0 / z_out))
        small_ref[...] = jnp.zeros_like(small_ref)
        small_ref[0:6, 0:elems] = source_ref[...].astype(F32)
        small_ref[8:14, 0:elems] = orient_ref[...].astype(F32)
        small_ref[16:22, 0:elems] = e_factor
        small_ref[24:30, 0:elems] = -h_factor
        small_ref[32:38, 0:elems] = -sign * z_out * e_factor
        small_ref[40:46, 0:elems] = -sign * h_factor / z_out
        small_ref[48:51, 0:elems] = scales / permit
        small_ref[56:59, 0:elems] = -scales / permea
        columns = jnp.transpose(small_ref[...])[0:elems]

        def col(group, index):
            return columns[:, 8 * group + index : 8 * group + index + 1]

        for face in range(6):
            rows = slice(face * elems, (face + 1) * elems)
            origin = col(0, face)
            own_ref[rows, :] = jnp.where(origin == code, 1.0, 0.0).astype(BF16)
            far_ref[rows, :] = jnp.where(origin == far_code, 1.0, 0.0).astype(BF16)
            coef_ref[0, rows, :] = jnp.where(low_half, col(2, face), col(3, face))
            coef_ref[1, rows, :] = jnp.where(low_half, col(4, face), col(5, face))
            coef_ref[2, rows, :] = jnp.where(origin < 0.0, jnp.where(low_half, 2.0, 0.0), 1.0)
            coef_ref[3, rows, :] = jnp.broadcast_to(col(1, face), (elems, 128))
        for axis in range(3):
            curl_ref[0, axis] = jnp.broadcast_to(col(6, axis), (elems, 128))
            curl_ref[1, axis] = jnp.broadcast_to(col(7, axis), (elems, 128))

    def stage(number):
        if number == 0:
            loads["fields"].wait()
            loads["pick"].wait()
        high, low = split(state_ref[...])
        both = mul(jnp.concatenate([high, low], axis=0), pick_ref[...])
        traces = both[0:faces] + both[faces:]
        half = lax.broadcasted_iota(jnp.int32, (3 * elems, 128), 1) < 64
        for axis in range(3):
            e_part = traces[0 : 3 * elems, axis * 128 : (axis + 1) * 128]
            h_part = traces[3 * elems :, axis * 128 : (axis + 1) * 128]
            near = jnp.where(half, e_part, swap(h_part))
            away = jnp.where(half, swap(e_part), h_part)
            for side, part in enumerate((near, away)):
                first = (2 * axis + side) * elems
                for dim in range(3):
                    table_ref[first : first + elems, dim * 128 : (dim + 1) * 128] = part[
                        dim * elems : (dim + 1) * elems
                    ]
        tab = jnp.concatenate(split(table_ref[...]), axis=1)
        sent = mul(choose_ref[...], tab)
        sent = sent[:, 0:384] + sent[:, 384:]
        copies = []
        for q, target in enumerate(targets):
            send_ref[number, q] = sent[q * slot : (q + 1) * slot]
        if number == 0:
            pl.semaphore_wait(barrier, len(targets))
        for q, target in enumerate(targets):
            copy = pltpu.make_async_remote_copy(
                src_ref=send_ref.at[number, q],
                dst_ref=recv_ref.at[number, q],
                send_sem=send_sem.at[number, q],
                recv_sem=recv_sem.at[number, q],
                device_id=target,
                device_id_type=MESH,
            )
            copy.start()
            copies.append(copy)

        if number == 0:
            prepare()
            loads["d0"].wait()
            loads["d12"].wait()
        active = jnp.concatenate([high[elems : 3 * elems], high[4 * elems :]], axis=0)
        active_low = jnp.concatenate([low[elems : 3 * elems], low[4 * elems :]], axis=0)
        slope0 = mul(jnp.concatenate([active, active_low], axis=0), d0_ref[0])
        slope0 = slope0[0 : 4 * elems] + slope0[4 * elems :] + mul(active, d0_ref[1])
        wide_in = jnp.concatenate(
            [
                jnp.concatenate([part[:, block * 128 : (block + 1) * 128] for block in range(4)], axis=0)
                for part in (high, low, high)
            ],
            axis=1,
        )
        slope12 = mul(wide_in, d12_ref[...])

        def slope(comp, axis):
            if axis == 0:
                place = 2 * (comp // 3) + comp % 3 - 1
                return slope0[place * elems : (place + 1) * elems]
            lanes = slice((axis - 1) * 128, axis * 128)
            return jnp.concatenate(
                [
                    slope12[(block * 6 + comp) * elems : (block * 6 + comp + 1) * elems, lanes]
                    for block in range(4)
                ],
                axis=1,
            )

        def factor(field, axis):
            return jnp.concatenate([curl_ref[field, axis]] * 4, axis=1)

        volume = []
        for field in range(2):
            other = 3 * (1 - field)
            for dim in range(3):
                one, two = (dim + 1) % 3, (dim + 2) % 3
                volume.append(
                    factor(field, one) * slope(other + two, one)
                    - factor(field, two) * slope(other + one, two)
                )
        volume = jnp.concatenate(volume, axis=0)

        got = mul(own_ref[...], tab)
        if number == 0:
            loads["turn"].wait()
            loads["lift"].wait()
        for copy in copies:
            copy.wait()
        beyond = jnp.concatenate(split(recv_ref[number].reshape(6 * slot, 384)), axis=1)
        got = (got + mul(far_ref[...], beyond)).astype(BF16)

        pieces = []
        for face in range(6):
            rows = slice(face * elems, (face + 1) * elems)
            for step in (1, 2):
                dim = (face // 2 + step) % 3
                pieces.append(
                    jnp.concatenate(
                        [
                            got[rows, dim * 128 : (dim + 1) * 128],
                            got[rows, 384 + dim * 128 : 384 + (dim + 1) * 128],
                        ],
                        axis=1,
                    )
                )
        turned = mul(jnp.concatenate(pieces, axis=0), turn_ref[...])

        faces_out = {}
        for face in range(6):
            axis = face // 2
            rows = slice(face * elems, (face + 1) * elems)
            flag = coef_ref[3, rows, :].astype(jnp.int32)
            jumps = []
            for step in (1, 2):
                dim = (axis + step) % 3
                first = (2 * face + step - 1) * elems
                forms = [turned[first : first + elems, o * 128 : (o + 1) * 128] for o in range(8)]
                for bit in (1, 2, 4):
                    chosen = (flag & bit) > 0
                    forms = [
                        jnp.where(chosen, forms[2 * o + 1], forms[2 * o]) for o in range(len(forms) // 2)
                    ]
                own_trace = table_ref[rows, dim * 128 : (dim + 1) * 128]
                jumps.append(own_trace * coef_ref[2, rows, :] - forms[0])
            straight = coef_ref[0, rows, :]
            crossed = coef_ref[1, rows, :]
            faces_out[face, (axis + 1) % 3] = straight * jumps[0] + crossed * swap(jumps[1])
            faces_out[face, (axis + 2) % 3] = straight * jumps[1] - crossed * swap(jumps[0])

        blank = jnp.zeros((elems, 128), F32)
        lines = []
        for field in range(2):
            for dim in range(3):
                line = []
                for axis in range(3):
                    if axis == dim:
                        line.append(blank)
                        continue
                    near, away = faces_out[2 * axis, dim], faces_out[2 * axis + 1, dim]
                    if field == 0:
                        line.append(jnp.where(low_half, near, swap(away)))
                    else:
                        line.append(jnp.where(low_half, swap(near), away))
                lines.append(jnp.concatenate(line, axis=1))
        lifted = mul(jnp.concatenate(split(jnp.concatenate(lines, axis=0)), axis=0), lift_ref[...])
        return volume + (lifted[0:faces] + lifted[faces:])

    first = stage(0)
    state = state_ref[...]
    base_ref[...] = state + (0.5 * TIME_STEP) * first
    state_ref[...] = state + TIME_STEP * first
    second = stage(1)
    out_ref[...] = base_ref[...] + (0.5 * TIME_STEP) * second


def local(
    fields,
    scales,
    class_table,
    material,
    neighbour_class,
    orientation,
    face_source,
    wide_send,
    bulk_send,
):
    elems = fields.shape[0]
    slot = wide_send.shape[3]
    faces = 6 * elems
    vmem = pl.BlockSpec(memory_space=pltpu.VMEM)
    hbm = pl.BlockSpec(memory_space=pltpu.HBM)
    matrices = constants()
    arguments = (
        fields.transpose(1, 0, 2).reshape(faces, 512),
        scales.T,
        class_table.T,
        material.reshape(1, elems),
        neighbour_class.T,
        orientation.T,
        face_source.T,
        wide_send,
        bulk_send,
    )
    result = pl.pallas_call(
        kernel,
        out_shape=jax.ShapeDtypeStruct((faces, 512), F32),
        in_specs=[hbm] * 14,
        out_specs=vmem,
        scratch_shapes=[
            pltpu.VMEM((faces, 512), F32),
            pltpu.VMEM((faces, 512), F32),
            *[pltpu.VMEM(matrix.shape, BF16) for matrix in matrices],
            *[pltpu.VMEM(value.shape, value.dtype) for value in arguments[1:]],
            pltpu.VMEM((128, 128), F32),
            pltpu.VMEM((faces, 384), F32),
            pltpu.VMEM((faces, faces), BF16),
            pltpu.VMEM((faces, 6 * slot), BF16),
            pltpu.VMEM((6 * slot, faces), BF16),
            pltpu.VMEM((4, faces, 128), F32),
            pltpu.VMEM((2, 3, elems, 128), F32),
            pltpu.VMEM((2, 6, slot, 384), F32),
            pltpu.VMEM((2, 6, slot, 384), F32),
            pltpu.SemaphoreType.DMA((14,)),
            pltpu.SemaphoreType.DMA((2, 6)),
            pltpu.SemaphoreType.DMA((2, 6)),
        ],
        compiler_params=pltpu.CompilerParams(
            collective_id=0, has_side_effects=True, vmem_limit_bytes=67043328
        ),
    )(*arguments, *matrices)
    return result.reshape(6, elems, 512).transpose(1, 0, 2)


def solution(mesh):
    in_specs = (
        P(("wide", "bulk"), None, None),
        P(("wide", "bulk"), None),
        P(),
        P(("wide", "bulk")),
        P(("wide", "bulk"), None),
        P(("wide", "bulk"), None),
        P(("wide", "bulk"), None),
        P("wide", "bulk", None, None),
        P("wide", "bulk", None, None),
    )
    out_specs = P(("wide", "bulk"), None, None)
    return jax.shard_map(local, mesh=mesh, in_specs=in_specs, out_specs=out_specs, check_vma=False)
```

```python
import functools

import jax
import jax.numpy as jnp
import numpy as np
from jax import lax
from jax.experimental import pallas as pl
from jax.experimental.pallas import tpu as pltpu
from jax.sharding import PartitionSpec as P

TIME_STEP = 0.005
LIFT_WEIGHT = 28.0
WIDE_OFFSETS = (-2, -1, 1, 2)
MESH = pl.DeviceIdType.MESH
F32 = jnp.float32
BF16 = jnp.bfloat16


def legendre_value(degree, point):
    previous = 1.0
    current = point
    for order in range(1, degree):
        following = ((2 * order + 1) * point * current - order * previous) / (order + 1)
        previous = current
        current = following
    return current


def gll_numpy():
    degree = 7
    points = [
        -1.0,
        -0.8717401485096066,
        -0.5917001814331423,
        -0.2092992179024789,
        0.2092992179024789,
        0.5917001814331423,
        0.8717401485096066,
        1.0,
    ]
    values = [legendre_value(degree, point) for point in points]
    matrix = np.zeros((degree + 1, degree + 1))
    for row_index in range(degree + 1):
        for col_index in range(degree + 1):
            if row_index != col_index:
                matrix[row_index, col_index] = values[row_index] / (
                    values[col_index] * (points[row_index] - points[col_index])
                )
    matrix[0, 0] = -degree * (degree + 1) / 4.0
    matrix[degree, degree] = degree * (degree + 1) / 4.0
    return matrix


def face_nodes():
    nodes = np.zeros((6, 64), dtype=np.int64)
    for face in range(6):
        axis_id = face // 2
        level = 7 * (face % 2)
        for place in range(64):
            outer = place // 8
            inner = place % 8
            if axis_id == 0:
                coords = (level, outer, inner)
            elif axis_id == 1:
                coords = (outer, level, inner)
            else:
                coords = (outer, inner, level)
            nodes[face, place] = 64 * coords[0] + 8 * coords[1] + coords[2]
    return nodes


def halves(matrix):
    high = np.asarray(matrix, dtype=np.float32).astype(jnp.bfloat16)
    low = (matrix - high.astype(np.float64)).astype(np.float32).astype(jnp.bfloat16)
    return high, low


def constants():
    pick = np.zeros((512, 384), dtype=np.float32)
    pick[face_nodes().reshape(-1), np.arange(384)] = 1.0
    turned = gll_numpy().T
    eye = np.eye(8)
    first = np.kron(turned, np.eye(64))
    second = np.kron(np.eye(2), np.kron(turned, eye))
    third = np.kron(np.eye(16), turned)
    d0 = np.stack(halves(first))
    d12 = np.concatenate([second, third], axis=1)
    high, low = halves(d12)
    d12 = np.concatenate([high, high, low], axis=0)
    turn = np.zeros((128, 8, 128), dtype=np.float32)
    for flag in range(8):
        for place in range(64):
            outer, inner = place // 8, place % 8
            outer = 7 - outer if flag & 1 else outer
            inner = 7 - inner if flag & 2 else inner
            source = inner * 8 + outer if flag & 4 else outer * 8 + inner
            for half in range(2):
                turn[half * 64 + source, flag, half * 64 + place] = 1.0
    turn = turn.reshape(128, 1024)
    turn = np.concatenate([turn, turn], axis=0)
    return (
        jnp.asarray(pick, dtype=BF16),
        jnp.asarray(pick.T, dtype=BF16),
        jnp.asarray(d0),
        jnp.asarray(d12),
        jnp.asarray(turn, dtype=BF16),
    )


def split(value):
    high = value.astype(BF16)
    low = (value - high.astype(F32)).astype(BF16)
    return high, low


def mul(left, right):
    return jnp.dot(left, right, preferred_element_type=F32)


def column(row):
    size = row.shape[1]
    shape = (size, size)
    same = lax.broadcasted_iota(jnp.int32, shape, 0) == lax.broadcasted_iota(jnp.int32, shape, 1)
    return jnp.sum(jnp.where(same, jnp.broadcast_to(row, shape), 0.0), axis=1, keepdims=True)


def swap(value):
    return pltpu.roll(value, 64, 1)


def kernel(
    fields_hbm,
    scales_hbm,
    class_hbm,
    material_hbm,
    neighbour_hbm,
    orient_hbm,
    source_hbm,
    wide_hbm,
    bulk_hbm,
    pick_hbm,
    lift_hbm,
    d0_hbm,
    d12_hbm,
    turn_hbm,
    out_ref,
    state_ref,
    base_ref,
    pick_ref,
    lift_ref,
    d0_ref,
    d12_ref,
    turn_ref,
    scales_ref,
    class_ref,
    material_ref,
    neighbour_ref,
    orient_ref,
    source_ref,
    wide_ref,
    bulk_ref,
    small_ref,
    table_ref,
    own_ref,
    far_ref,
    choose_ref,
    coef_ref,
    curl_ref,
    send_ref,
    recv_ref,
    load_sem,
    send_sem,
    recv_sem,
):
    elems = material_hbm.shape[1]
    faces = 6 * elems
    slot = wide_hbm.shape[3]
    wide_id, bulk_id = lax.axis_index("wide"), lax.axis_index("bulk")
    n_wide, n_bulk = lax.axis_size("wide"), lax.axis_size("bulk")
    targets = [(lax.rem(wide_id + offset + n_wide, n_wide), bulk_id) for offset in WIDE_OFFSETS]
    targets.append((wide_id, lax.rem(bulk_id + 1, n_bulk)))
    targets.append((wide_id, lax.rem(bulk_id + n_bulk - 1, n_bulk)))

    barrier = pltpu.get_barrier_semaphore()
    for target in targets:
        pl.semaphore_signal(barrier, inc=1, device_id=target, device_id_type=MESH)

    loads = {}
    for place, (name, source, target) in enumerate(
        (
            ("wide", wide_hbm, wide_ref),
            ("bulk", bulk_hbm, bulk_ref),
            ("fields", fields_hbm, state_ref),
            ("pick", pick_hbm, pick_ref),
            ("scales", scales_hbm, scales_ref),
            ("class", class_hbm, class_ref),
            ("material", material_hbm, material_ref),
            ("neighbour", neighbour_hbm, neighbour_ref),
            ("orient", orient_hbm, orient_ref),
            ("source", source_hbm, source_ref),
            ("d0", d0_hbm, d0_ref),
            ("d12", d12_hbm, d12_ref),
            ("turn", turn_hbm, turn_ref),
            ("lift", lift_hbm, lift_ref),
        )
    ):
        loads[name] = pltpu.make_async_copy(source, target, load_sem.at[place])
        loads[name].start()

    spot = lax.broadcasted_iota(jnp.int32, (1, faces), 1)
    part = jnp.zeros((1, faces), jnp.int32)
    for face in range(1, 6):
        part = part + jnp.where(spot >= face * elems, 1, 0)
    code = (6 * (spot - elems * part) + part).astype(F32)
    loads["wide"].wait()
    loads["bulk"].wait()
    wide_rows = wide_ref[0, 0].astype(F32)
    bulk_rows = bulk_ref[0, 0].astype(F32)
    order = [wide_rows[q : q + 1] for q in range(4)] + [bulk_rows[1:2], bulk_rows[0:1]]
    for q, row in enumerate(order):
        choose_ref[q * slot : (q + 1) * slot, :] = jnp.where(column(row) == code, 1.0, 0.0).astype(BF16)

    low_half = lax.broadcasted_iota(jnp.int32, (elems, 128), 1) < 64

    def prepare():
        for name in ("scales", "class", "material", "neighbour", "orient", "source"):
            loads[name].wait()
        far_code = (lax.broadcasted_iota(jnp.int32, (elems, 6 * slot), 1) + faces).astype(F32)
        material = material_ref[...]
        neighbour = neighbour_ref[...]
        table = class_ref[...]
        imped = jnp.sqrt(table[1:2, :] / table[0:1, :])
        permit = jnp.zeros((1, elems), F32)
        permea = jnp.zeros((1, elems), F32)
        own_imp = jnp.zeros((1, elems), F32)
        z_out = jnp.zeros((6, elems), F32)
        for entry in range(class_ref.shape[1]):
            hit = material == entry
            permit = permit + jnp.where(hit, table[0:1, entry : entry + 1], 0.0)
            permea = permea + jnp.where(hit, table[1:2, entry : entry + 1], 0.0)
            own_imp = own_imp + jnp.where(hit, imped[:, entry : entry + 1], 0.0)
            z_out = z_out + jnp.where(neighbour == entry, imped[:, entry : entry + 1], 0.0)
        side = lax.broadcasted_iota(jnp.int32, (6, elems), 0)
        sign = jnp.where((side & 1) > 0, 1.0, -1.0)
        scales = scales_ref[...]
        lift = LIFT_WEIGHT * jnp.where(side < 2, scales[0:1], jnp.where(side < 4, scales[1:2], scales[2:3]))
        e_factor = -lift / (permit * (own_imp + z_out))
        h_factor = lift / (permea * (1.0 / own_imp + 1.0 / z_out))
        small_ref[...] = jnp.zeros_like(small_ref)
        small_ref[0:6, 0:elems] = source_ref[...].astype(F32)
        small_ref[8:14, 0:elems] = orient_ref[...].astype(F32)
        small_ref[16:22, 0:elems] = e_factor
        small_ref[24:30, 0:elems] = -h_factor
        small_ref[32:38, 0:elems] = -sign * z_out * e_factor
        small_ref[40:46, 0:elems] = -sign * h_factor / z_out
        small_ref[48:51, 0:elems] = scales / permit
        small_ref[56:59, 0:elems] = -scales / permea
        columns = jnp.transpose(small_ref[...])[0:elems]

        def col(group, index):
            return columns[:, 8 * group + index : 8 * group + index + 1]

        for face in range(6):
            rows = slice(face * elems, (face + 1) * elems)
            origin = col(0, face)
            own_ref[rows, :] = jnp.where(origin == code, 1.0, 0.0).astype(BF16)
            far_ref[rows, :] = jnp.where(origin == far_code, 1.0, 0.0).astype(BF16)
            coef_ref[0, rows, :] = jnp.where(low_half, col(2, face), col(3, face))
            coef_ref[1, rows, :] = jnp.where(low_half, col(4, face), col(5, face))
            coef_ref[2, rows, :] = jnp.where(origin < 0.0, jnp.where(low_half, 2.0, 0.0), 1.0)
            coef_ref[3, rows, :] = jnp.broadcast_to(col(1, face), (elems, 128))
        for axis in range(3):
            curl_ref[0, axis] = jnp.broadcast_to(col(6, axis), (elems, 128))
            curl_ref[1, axis] = jnp.broadcast_to(col(7, axis), (elems, 128))

    def stage(number):
        if number == 0:
            loads["fields"].wait()
            loads["pick"].wait()
        high, low = split(state_ref[...])
        both = mul(jnp.concatenate([high, low], axis=0), pick_ref[...])
        traces = both[0:faces] + both[faces:]
        half = lax.broadcasted_iota(jnp.int32, (3 * elems, 128), 1) < 64
        for axis in range(3):
            e_part = traces[0 : 3 * elems, axis * 128 : (axis + 1) * 128]
            h_part = traces[3 * elems :, axis * 128 : (axis + 1) * 128]
            near = jnp.where(half, e_part, swap(h_part))
            away = jnp.where(half, swap(e_part), h_part)
            for side, part in enumerate((near, away)):
                first = (2 * axis + side) * elems
                for dim in range(3):
                    table_ref[first : first + elems, dim * 128 : (dim + 1) * 128] = part[
                        dim * elems : (dim + 1) * elems
                    ]
        tab = jnp.concatenate(split(table_ref[...]), axis=1)
        sent = mul(choose_ref[...], tab)
        sent = sent[:, 0:384] + sent[:, 384:]
        copies = []
        for q, target in enumerate(targets):
            send_ref[number, q] = sent[q * slot : (q + 1) * slot]
        if number == 0:
            pl.semaphore_wait(barrier, len(targets))
        for q, target in enumerate(targets):
            copy = pltpu.make_async_remote_copy(
                src_ref=send_ref.at[number, q],
                dst_ref=recv_ref.at[number, q],
                send_sem=send_sem.at[number, q],
                recv_sem=recv_sem.at[number, q],
                device_id=target,
                device_id_type=MESH,
            )
            copy.start()
            copies.append(copy)

        if number == 0:
            prepare()
            loads["d0"].wait()
            loads["d12"].wait()
        active = jnp.concatenate([high[elems : 3 * elems], high[4 * elems :]], axis=0)
        active_low = jnp.concatenate([low[elems : 3 * elems], low[4 * elems :]], axis=0)
        slope0 = mul(jnp.concatenate([active, active_low], axis=0), d0_ref[0])
        slope0 = slope0[0 : 4 * elems] + slope0[4 * elems :] + mul(active, d0_ref[1])
        wide_in = jnp.concatenate(
            [
                jnp.concatenate([part[:, block * 128 : (block + 1) * 128] for block in range(4)], axis=0)
                for part in (high, low, high)
            ],
            axis=1,
        )
        slope12 = mul(wide_in, d12_ref[...])

        def slope(comp, axis):
            if axis == 0:
                place = 2 * (comp // 3) + comp % 3 - 1
                return slope0[place * elems : (place + 1) * elems]
            lanes = slice((axis - 1) * 128, axis * 128)
            return jnp.concatenate(
                [
                    slope12[(block * 6 + comp) * elems : (block * 6 + comp + 1) * elems, lanes]
                    for block in range(4)
                ],
                axis=1,
            )

        def factor(field, axis):
            return jnp.concatenate([curl_ref[field, axis]] * 4, axis=1)

        volume = []
        for field in range(2):
            other = 3 * (1 - field)
            for dim in range(3):
                one, two = (dim + 1) % 3, (dim + 2) % 3
                volume.append(
                    factor(field, one) * slope(other + two, one)
                    - factor(field, two) * slope(other + one, two)
                )
        volume = jnp.concatenate(volume, axis=0)

        got = mul(own_ref[...], tab)
        if number == 0:
            loads["turn"].wait()
            loads["lift"].wait()
        for copy in copies:
            copy.wait()
        beyond = jnp.concatenate(split(recv_ref[number].reshape(6 * slot, 384)), axis=1)
        got = (got + mul(far_ref[...], beyond)).astype(BF16)

        pieces = []
        for face in range(6):
            rows = slice(face * elems, (face + 1) * elems)
            for step in (1, 2):
                dim = (face // 2 + step) % 3
                pieces.append(
                    jnp.concatenate(
                        [
                            got[rows, dim * 128 : (dim + 1) * 128],
                            got[rows, 384 + dim * 128 : 384 + (dim + 1) * 128],
                        ],
                        axis=1,
                    )
                )
        turned = mul(jnp.concatenate(pieces, axis=0), turn_ref[...])

        faces_out = {}
        for face in range(6):
            axis = face // 2
            rows = slice(face * elems, (face + 1) * elems)
            flag = coef_ref[3, rows, :].astype(jnp.int32)
            jumps = []
            for step in (1, 2):
                dim = (axis + step) % 3
                first = (2 * face + step - 1) * elems
                forms = [turned[first : first + elems, o * 128 : (o + 1) * 128] for o in range(8)]
                for bit in (1, 2, 4):
                    chosen = (flag & bit) > 0
                    forms = [
                        jnp.where(chosen, forms[2 * o + 1], forms[2 * o]) for o in range(len(forms) // 2)
                    ]
                own_trace = table_ref[rows, dim * 128 : (dim + 1) * 128]
                jumps.append(own_trace * coef_ref[2, rows, :] - forms[0])
            straight = coef_ref[0, rows, :]
            crossed = coef_ref[1, rows, :]
            faces_out[face, (axis + 1) % 3] = straight * jumps[0] + crossed * swap(jumps[1])
            faces_out[face, (axis + 2) % 3] = straight * jumps[1] - crossed * swap(jumps[0])

        blank = jnp.zeros((elems, 128), F32)
        lines = []
        for field in range(2):
            for dim in range(3):
                line = []
                for axis in range(3):
                    if axis == dim:
                        line.append(blank)
                        continue
                    near, away = faces_out[2 * axis, dim], faces_out[2 * axis + 1, dim]
                    if field == 0:
                        line.append(jnp.where(low_half, near, swap(away)))
                    else:
                        line.append(jnp.where(low_half, swap(near), away))
                lines.append(jnp.concatenate(line, axis=1))
        lifted = mul(jnp.concatenate(split(jnp.concatenate(lines, axis=0)), axis=0), lift_ref[...])
        return volume + (lifted[0:faces] + lifted[faces:])

    first = stage(0)
    state = state_ref[...]
    base_ref[...] = state + (0.5 * TIME_STEP) * first
    state_ref[...] = state + TIME_STEP * first
    second = stage(1)
    out_ref[...] = base_ref[...] + (0.5 * TIME_STEP) * second


def local(
    fields,
    scales,
    class_table,
    material,
    neighbour_class,
    orientation,
    face_source,
    wide_send,
    bulk_send,
):
    elems = fields.shape[0]
    slot = wide_send.shape[3]
    faces = 6 * elems
    vmem = pl.BlockSpec(memory_space=pltpu.VMEM)
    hbm = pl.BlockSpec(memory_space=pltpu.HBM)
    matrices = constants()
    arguments = (
        fields.transpose(1, 0, 2).reshape(faces, 512),
        scales.T,
        class_table.T,
        material.reshape(1, elems),
        neighbour_class.T,
        orientation.T,
        face_source.T,
        wide_send,
        bulk_send,
    )
    result = pl.pallas_call(
        kernel,
        out_shape=jax.ShapeDtypeStruct((faces, 512), F32),
        in_specs=[hbm] * 14,
        out_specs=vmem,
        scratch_shapes=[
            pltpu.VMEM((faces, 512), F32),
            pltpu.VMEM((faces, 512), F32),
            *[pltpu.VMEM(matrix.shape, BF16) for matrix in matrices],
            *[pltpu.VMEM(value.shape, value.dtype) for value in arguments[1:]],
            pltpu.VMEM((128, 128), F32),
            pltpu.VMEM((faces, 384), F32),
            pltpu.VMEM((faces, faces), BF16),
            pltpu.VMEM((faces, 6 * slot), BF16),
            pltpu.VMEM((6 * slot, faces), BF16),
            pltpu.VMEM((4, faces, 128), F32),
            pltpu.VMEM((2, 3, elems, 128), F32),
            pltpu.VMEM((2, 6, slot, 384), F32),
            pltpu.VMEM((2, 6, slot, 384), F32),
            pltpu.SemaphoreType.DMA((14,)),
            pltpu.SemaphoreType.DMA((2, 6)),
            pltpu.SemaphoreType.DMA((2, 6)),
        ],
        compiler_params=pltpu.CompilerParams(
            collective_id=0, has_side_effects=True, vmem_limit_bytes=48 * 1024 * 1024
        ),
    )(*[pltpu.with_memory_space_constraint(value, pltpu.HBM) for value in (*arguments, *matrices)])
    return result.reshape(6, elems, 512).transpose(1, 0, 2)


def solution(mesh):
    in_specs = (
        P(("wide", "bulk"), None, None),
        P(("wide", "bulk"), None),
        P(),
        P(("wide", "bulk")),
        P(("wide", "bulk"), None),
        P(("wide", "bulk"), None),
        P(("wide", "bulk"), None),
        P("wide", "bulk", None, None),
        P("wide", "bulk", None, None),
    )
    out_specs = P(("wide", "bulk"), None, None)
    return jax.shard_map(local, mesh=mesh, in_specs=in_specs, out_specs=out_specs, check_vma=False)
```

```python
import functools

import jax
import jax.numpy as jnp
import numpy as np
from jax import lax
from jax.experimental import pallas as pl
from jax.experimental.pallas import tpu as pltpu
from jax.sharding import PartitionSpec as P

TIME_STEP = 0.005
LIFT_WEIGHT = 28.0
WIDE_OFFSETS = (-2, -1, 1, 2)
MESH = pl.DeviceIdType.MESH
F32 = jnp.float32
BF16 = jnp.bfloat16


def legendre_value(degree, point):
    previous = 1.0
    current = point
    for order in range(1, degree):
        following = ((2 * order + 1) * point * current - order * previous) / (order + 1)
        previous = current
        current = following
    return current


def gll_numpy():
    degree = 7
    points = [
        -1.0,
        -0.8717401485096066,
        -0.5917001814331423,
        -0.2092992179024789,
        0.2092992179024789,
        0.5917001814331423,
        0.8717401485096066,
        1.0,
    ]
    values = [legendre_value(degree, point) for point in points]
    matrix = np.zeros((degree + 1, degree + 1))
    for row_index in range(degree + 1):
        for col_index in range(degree + 1):
            if row_index != col_index:
                matrix[row_index, col_index] = values[row_index] / (
                    values[col_index] * (points[row_index] - points[col_index])
                )
    matrix[0, 0] = -degree * (degree + 1) / 4.0
    matrix[degree, degree] = degree * (degree + 1) / 4.0
    return matrix


def face_nodes():
    nodes = np.zeros((6, 64), dtype=np.int64)
    for face in range(6):
        axis_id = face // 2
        level = 7 * (face % 2)
        for place in range(64):
            outer = place // 8
            inner = place % 8
            if axis_id == 0:
                coords = (level, outer, inner)
            elif axis_id == 1:
                coords = (outer, level, inner)
            else:
                coords = (outer, inner, level)
            nodes[face, place] = 64 * coords[0] + 8 * coords[1] + coords[2]
    return nodes


def halves(matrix):
    high = np.asarray(matrix, dtype=np.float32).astype(jnp.bfloat16)
    low = (matrix - high.astype(np.float64)).astype(np.float32).astype(jnp.bfloat16)
    return high, low


def constants():
    pick = np.zeros((512, 384), dtype=np.float32)
    pick[face_nodes().reshape(-1), np.arange(384)] = 1.0
    turned = gll_numpy().T
    eye = np.eye(8)
    first = np.kron(turned, np.eye(64))
    second = np.kron(np.eye(2), np.kron(turned, eye))
    third = np.kron(np.eye(16), turned)
    d0 = np.stack(halves(first))
    d12 = np.concatenate([second, third], axis=1)
    high, low = halves(d12)
    d12 = np.concatenate([high, high, low], axis=0)
    turn = np.zeros((128, 8, 128), dtype=np.float32)
    for flag in range(8):
        for place in range(64):
            outer, inner = place // 8, place % 8
            outer = 7 - outer if flag & 1 else outer
            inner = 7 - inner if flag & 2 else inner
            source = inner * 8 + outer if flag & 4 else outer * 8 + inner
            for half in range(2):
                turn[half * 64 + source, flag, half * 64 + place] = 1.0
    turn = turn.reshape(128, 1024)
    turn = np.concatenate([turn, turn], axis=0)
    return (
        jnp.asarray(pick[:, 128:], dtype=BF16),
        jnp.asarray(pick[:, 128:].T, dtype=BF16),
        jnp.asarray(d0),
        jnp.asarray(d12),
        jnp.asarray(turn, dtype=BF16),
    )


def split(value):
    high = value.astype(BF16)
    low = (value - high.astype(F32)).astype(BF16)
    return high, low


def mul(left, right):
    return jnp.dot(left, right, preferred_element_type=F32)


def column(row):
    size = row.shape[1]
    shape = (size, size)
    same = lax.broadcasted_iota(jnp.int32, shape, 0) == lax.broadcasted_iota(jnp.int32, shape, 1)
    return jnp.sum(jnp.where(same, jnp.broadcast_to(row, shape), 0.0), axis=1, keepdims=True)


def swap(value):
    return pltpu.roll(value, 64, 1)


def kernel(
    fields_hbm,
    scales_hbm,
    class_hbm,
    material_hbm,
    neighbour_hbm,
    orient_hbm,
    source_hbm,
    wide_hbm,
    bulk_hbm,
    pick_hbm,
    lift_hbm,
    d0_hbm,
    d12_hbm,
    turn_hbm,
    out_ref,
    state_ref,
    base_ref,
    pick_ref,
    lift_ref,
    d0_ref,
    d12_ref,
    turn_ref,
    scales_ref,
    class_ref,
    material_ref,
    neighbour_ref,
    orient_ref,
    source_ref,
    wide_ref,
    bulk_ref,
    small_ref,
    table_ref,
    own_ref,
    far_ref,
    choose_ref,
    coef_ref,
    curl_ref,
    send_ref,
    recv_ref,
    load_sem,
    send_sem,
    recv_sem,
):
    elems = material_hbm.shape[1]
    faces = 6 * elems
    slot = wide_hbm.shape[3]
    wide_id, bulk_id = lax.axis_index("wide"), lax.axis_index("bulk")
    n_wide, n_bulk = lax.axis_size("wide"), lax.axis_size("bulk")
    targets = [(lax.rem(wide_id + offset + n_wide, n_wide), bulk_id) for offset in WIDE_OFFSETS]
    targets.append((wide_id, lax.rem(bulk_id + 1, n_bulk)))
    targets.append((wide_id, lax.rem(bulk_id + n_bulk - 1, n_bulk)))

    barrier = pltpu.get_barrier_semaphore()
    for target in targets:
        pl.semaphore_signal(barrier, inc=1, device_id=target, device_id_type=MESH)

    loads = {}
    for place, (name, source, target) in enumerate(
        (
            ("wide", wide_hbm, wide_ref),
            ("bulk", bulk_hbm, bulk_ref),
            ("fields", fields_hbm, state_ref),
            ("pick", pick_hbm, pick_ref),
            ("scales", scales_hbm, scales_ref),
            ("class", class_hbm, class_ref),
            ("material", material_hbm, material_ref),
            ("neighbour", neighbour_hbm, neighbour_ref),
            ("orient", orient_hbm, orient_ref),
            ("source", source_hbm, source_ref),
            ("d0", d0_hbm, d0_ref),
            ("d12", d12_hbm, d12_ref),
            ("turn", turn_hbm, turn_ref),
            ("lift", lift_hbm, lift_ref),
        )
    ):
        loads[name] = pltpu.make_async_copy(source, target, load_sem.at[place])
        if name not in ("d0", "d12", "turn", "lift"):
            loads[name].start()

    spot = lax.broadcasted_iota(jnp.int32, (1, faces), 1)
    part = jnp.zeros((1, faces), jnp.int32)
    for face in range(1, 6):
        part = part + jnp.where(spot >= face * elems, 1, 0)
    code = (6 * (spot - elems * part) + part).astype(F32)
    loads["wide"].wait()
    loads["bulk"].wait()
    wide_rows = wide_ref[0, 0].astype(F32)
    bulk_rows = bulk_ref[0, 0].astype(F32)
    order = [wide_rows[q : q + 1] for q in range(4)] + [bulk_rows[1:2], bulk_rows[0:1]]
    for q, row in enumerate(order):
        choose_ref[q * slot : (q + 1) * slot, :] = jnp.where(column(row) == code, 1.0, 0.0).astype(BF16)

    low_half = lax.broadcasted_iota(jnp.int32, (elems, 128), 1) < 64

    def prepare():
        for name in ("scales", "class", "material", "neighbour", "orient", "source"):
            loads[name].wait()
        far_code = (lax.broadcasted_iota(jnp.int32, (elems, 6 * slot), 1) + faces).astype(F32)
        material = material_ref[...]
        neighbour = neighbour_ref[...]
        table = class_ref[...]
        imped = jnp.sqrt(table[1:2, :] / table[0:1, :])
        permit = jnp.zeros((1, elems), F32)
        permea = jnp.zeros((1, elems), F32)
        own_imp = jnp.zeros((1, elems), F32)
        z_out = jnp.zeros((6, elems), F32)
        for entry in range(class_ref.shape[1]):
            hit = material == entry
            permit = permit + jnp.where(hit, table[0:1, entry : entry + 1], 0.0)
            permea = permea + jnp.where(hit, table[1:2, entry : entry + 1], 0.0)
            own_imp = own_imp + jnp.where(hit, imped[:, entry : entry + 1], 0.0)
            z_out = z_out + jnp.where(neighbour == entry, imped[:, entry : entry + 1], 0.0)
        side = lax.broadcasted_iota(jnp.int32, (6, elems), 0)
        sign = jnp.where((side & 1) > 0, 1.0, -1.0)
        scales = scales_ref[...]
        lift = LIFT_WEIGHT * jnp.where(side < 2, scales[0:1], jnp.where(side < 4, scales[1:2], scales[2:3]))
        e_factor = -lift / (permit * (own_imp + z_out))
        h_factor = lift / (permea * (1.0 / own_imp + 1.0 / z_out))
        small_ref[...] = jnp.zeros_like(small_ref)
        small_ref[0:6, 0:elems] = source_ref[...].astype(F32)
        small_ref[8:14, 0:elems] = orient_ref[...].astype(F32)
        small_ref[16:22, 0:elems] = e_factor
        small_ref[24:30, 0:elems] = -h_factor
        small_ref[32:38, 0:elems] = -sign * z_out * e_factor
        small_ref[40:46, 0:elems] = -sign * h_factor / z_out
        small_ref[48:51, 0:elems] = scales / permit
        small_ref[56:59, 0:elems] = -scales / permea
        columns = jnp.transpose(small_ref[...])[0:elems]

        def col(group, index):
            return columns[:, 8 * group + index : 8 * group + index + 1]

        for face in range(6):
            rows = slice(face * elems, (face + 1) * elems)
            origin = col(0, face)
            own_ref[rows, :] = jnp.where(origin == code, 1.0, 0.0).astype(BF16)
            far_ref[rows, :] = jnp.where(origin == far_code, 1.0, 0.0).astype(BF16)
            coef_ref[0, rows, :] = jnp.where(low_half, col(2, face), col(3, face))
            coef_ref[1, rows, :] = jnp.where(low_half, col(4, face), col(5, face))
            coef_ref[2, rows, :] = jnp.where(origin < 0.0, jnp.where(low_half, 2.0, 0.0), 1.0)
            coef_ref[3, rows, :] = jnp.broadcast_to(col(1, face), (elems, 128))
        for axis in range(3):
            curl_ref[0, axis] = jnp.broadcast_to(col(6, axis), (elems, 128))
            curl_ref[1, axis] = jnp.broadcast_to(col(7, axis), (elems, 128))

    def stage(number):
        if number == 0:
            loads["fields"].wait()
            loads["pick"].wait()
            for name in ("d0", "d12", "turn", "lift"):
                loads[name].start()
        state = state_ref[...]
        high, low = split(state)
        both = mul(jnp.concatenate([high, low], axis=0), pick_ref[...])
        every = lax.broadcasted_iota(jnp.int32, (faces, 128), 1) < 64
        ends = jnp.where(every, state[:, 0:128], state[:, 384:512])
        traces = jnp.concatenate([ends, both[0:faces] + both[faces:]], axis=1)
        half = lax.broadcasted_iota(jnp.int32, (3 * elems, 128), 1) < 64
        for axis in range(3):
            e_part = traces[0 : 3 * elems, axis * 128 : (axis + 1) * 128]
            h_part = traces[3 * elems :, axis * 128 : (axis + 1) * 128]
            near = jnp.where(half, e_part, swap(h_part))
            away = jnp.where(half, swap(e_part), h_part)
            for side, part in enumerate((near, away)):
                first = (2 * axis + side) * elems
                for dim in range(3):
                    table_ref[first : first + elems, dim * 128 : (dim + 1) * 128] = part[
                        dim * elems : (dim + 1) * elems
                    ]
        tab = jnp.concatenate(split(table_ref[...]), axis=1)
        sent = mul(choose_ref[...], tab)
        sent = sent[:, 0:384] + sent[:, 384:]
        copies = []
        for q, target in enumerate(targets):
            send_ref[number, q] = sent[q * slot : (q + 1) * slot]
        if number == 0:
            pl.semaphore_wait(barrier, len(targets))
        for q in (1, 2, 0, 3, 4, 5):
            target = targets[q]
            copy = pltpu.make_async_remote_copy(
                src_ref=send_ref.at[number, q],
                dst_ref=recv_ref.at[number, q],
                send_sem=send_sem.at[number, q],
                recv_sem=recv_sem.at[number, q],
                device_id=target,
                device_id_type=MESH,
            )
            copy.start()
            copies.append(copy)

        if number == 0:
            prepare()
            loads["d0"].wait()
            loads["d12"].wait()
        active = jnp.concatenate([high[elems : 3 * elems], high[4 * elems :]], axis=0)
        active_low = jnp.concatenate([low[elems : 3 * elems], low[4 * elems :]], axis=0)
        slope0 = mul(jnp.concatenate([active, active_low], axis=0), d0_ref[0])
        slope0 = slope0[0 : 4 * elems] + slope0[4 * elems :] + mul(active, d0_ref[1])
        wide_in = jnp.concatenate(
            [
                jnp.concatenate([part[:, block * 128 : (block + 1) * 128] for block in range(4)], axis=0)
                for part in (high, low, high)
            ],
            axis=1,
        )
        slope12 = mul(wide_in, d12_ref[...])

        def slope(comp, axis):
            if axis == 0:
                place = 2 * (comp // 3) + comp % 3 - 1
                return slope0[place * elems : (place + 1) * elems]
            lanes = slice((axis - 1) * 128, axis * 128)
            return jnp.concatenate(
                [
                    slope12[(block * 6 + comp) * elems : (block * 6 + comp + 1) * elems, lanes]
                    for block in range(4)
                ],
                axis=1,
            )

        def factor(field, axis):
            return jnp.concatenate([curl_ref[field, axis]] * 4, axis=1)

        volume = []
        for field in range(2):
            other = 3 * (1 - field)
            for dim in range(3):
                one, two = (dim + 1) % 3, (dim + 2) % 3
                volume.append(
                    factor(field, one) * slope(other + two, one)
                    - factor(field, two) * slope(other + one, two)
                )
        volume = jnp.concatenate(volume, axis=0)

        got = mul(own_ref[...], tab)
        if number == 0:
            loads["turn"].wait()
            loads["lift"].wait()
        for copy in copies:
            copy.wait()
        beyond = jnp.concatenate(split(recv_ref[number].reshape(6 * slot, 384)), axis=1)
        got = (got + mul(far_ref[...], beyond)).astype(BF16)

        pieces = []
        for face in range(6):
            rows = slice(face * elems, (face + 1) * elems)
            for step in (1, 2):
                dim = (face // 2 + step) % 3
                pieces.append(
                    jnp.concatenate(
                        [
                            got[rows, dim * 128 : (dim + 1) * 128],
                            got[rows, 384 + dim * 128 : 384 + (dim + 1) * 128],
                        ],
                        axis=1,
                    )
                )
        turned = mul(jnp.concatenate(pieces, axis=0), turn_ref[...])

        faces_out = {}
        for face in range(6):
            axis = face // 2
            rows = slice(face * elems, (face + 1) * elems)
            flag = coef_ref[3, rows, :].astype(jnp.int32)
            jumps = []
            for step in (1, 2):
                dim = (axis + step) % 3
                first = (2 * face + step - 1) * elems
                forms = [turned[first : first + elems, o * 128 : (o + 1) * 128] for o in range(8)]
                for bit in (1, 2, 4):
                    chosen = (flag & bit) > 0
                    forms = [
                        jnp.where(chosen, forms[2 * o + 1], forms[2 * o]) for o in range(len(forms) // 2)
                    ]
                own_trace = table_ref[rows, dim * 128 : (dim + 1) * 128]
                jumps.append(own_trace * coef_ref[2, rows, :] - forms[0])
            straight = coef_ref[0, rows, :]
            crossed = coef_ref[1, rows, :]
            faces_out[face, (axis + 1) % 3] = straight * jumps[0] + crossed * swap(jumps[1])
            faces_out[face, (axis + 2) % 3] = straight * jumps[1] - crossed * swap(jumps[0])

        blank = jnp.zeros((elems, 128), F32)
        lines = []
        for field in range(2):
            for dim in range(3):
                line = []
                for axis in range(3):
                    if axis == dim:
                        line.append(blank)
                        continue
                    near, away = faces_out[2 * axis, dim], faces_out[2 * axis + 1, dim]
                    if field == 0:
                        line.append(jnp.where(low_half, near, swap(away)))
                    else:
                        line.append(jnp.where(low_half, swap(near), away))
                lines.append(jnp.concatenate(line, axis=1))
        lines = jnp.concatenate(lines, axis=0)
        lifted = mul(jnp.concatenate(split(lines[:, 128:]), axis=0), lift_ref[...])
        ends = lines[:, 0:128]
        none = jnp.zeros_like(ends)
        ends = jnp.concatenate([jnp.where(every, ends, 0.0), none, none, jnp.where(every, 0.0, ends)], axis=1)
        return volume + ends + (lifted[0:faces] + lifted[faces:])

    first = stage(0)
    state = state_ref[...]
    base_ref[...] = state + (0.5 * TIME_STEP) * first
    state_ref[...] = state + TIME_STEP * first
    second = stage(1)
    out_ref[...] = base_ref[...] + (0.5 * TIME_STEP) * second


def local(
    fields,
    scales,
    class_table,
    material,
    neighbour_class,
    orientation,
    face_source,
    wide_send,
    bulk_send,
):
    elems = fields.shape[0]
    slot = wide_send.shape[3]
    faces = 6 * elems
    vmem = pl.BlockSpec(memory_space=pltpu.VMEM)
    hbm = pl.BlockSpec(memory_space=pltpu.HBM)
    matrices = constants()
    arguments = (
        fields.transpose(1, 0, 2).reshape(faces, 512),
        scales.T,
        class_table.T,
        material.reshape(1, elems),
        neighbour_class.T,
        orientation.T,
        face_source.T,
        wide_send,
        bulk_send,
    )
    result = pl.pallas_call(
        kernel,
        out_shape=jax.ShapeDtypeStruct((faces, 512), F32),
        in_specs=[hbm] * 14,
        out_specs=vmem,
        scratch_shapes=[
            pltpu.VMEM((faces, 512), F32),
            pltpu.VMEM((faces, 512), F32),
            *[pltpu.VMEM(matrix.shape, BF16) for matrix in matrices],
            *[pltpu.VMEM(value.shape, value.dtype) for value in arguments[1:]],
            pltpu.VMEM((128, 128), F32),
            pltpu.VMEM((faces, 384), F32),
            pltpu.VMEM((faces, faces), BF16),
            pltpu.VMEM((faces, 6 * slot), BF16),
            pltpu.VMEM((6 * slot, faces), BF16),
            pltpu.VMEM((4, faces, 128), F32),
            pltpu.VMEM((2, 3, elems, 128), F32),
            pltpu.VMEM((2, 6, slot, 384), F32),
            pltpu.VMEM((2, 6, slot, 384), F32),
            pltpu.SemaphoreType.DMA((14,)),
            pltpu.SemaphoreType.DMA((2, 6)),
            pltpu.SemaphoreType.DMA((2, 6)),
        ],
        compiler_params=pltpu.CompilerParams(
            collective_id=0, has_side_effects=True, vmem_limit_bytes=48 * 1024 * 1024
        ),
    )(*[pltpu.with_memory_space_constraint(value, pltpu.HBM) for value in (*arguments, *matrices)])
    return result.reshape(6, elems, 512).transpose(1, 0, 2)


def solution(mesh):
    in_specs = (
        P(("wide", "bulk"), None, None),
        P(("wide", "bulk"), None),
        P(),
        P(("wide", "bulk")),
        P(("wide", "bulk"), None),
        P(("wide", "bulk"), None),
        P(("wide", "bulk"), None),
        P("wide", "bulk", None, None),
        P("wide", "bulk", None, None),
    )
    out_specs = P(("wide", "bulk"), None, None)
    return jax.shard_map(local, mesh=mesh, in_specs=in_specs, out_specs=out_specs, check_vma=False)
```
